256 devices in a mesh: pair: 64 (over y, z, x_hi), az: 2 (over x_lo), rg: 2 (over core).
Axes of the slice: x: 4 (x_hi: 2, x_lo: 2; x = x_hi * 2 + x_lo), y: 4, z: 8, core: 2. Of those that a mesh axis runs over, the one named last changes fastest.
Arguments:
- acquisitions: bfloat16 [1024, 2, 40, 5120], P('pair', None, 'az', 'rg'), may hold values from -8 to 8
- reference_index: int32 [256], P('pair'), may hold values from 0 to 1022, as said below
- secondary_index: int32 [256], P('pair'), may hold values from 1 to 1023, as said below
- pair_count: int32 [64], P('pair'), may hold values from 1 to 4, 160 in all
Outputs:
- interferogram: float32 [256, 2, 8, 256], P('pair', None, 'az', 'rg')
- coherence: float32 [256, 8, 256], P('pair', 'az', 'rg')
The draws below stay inside these ranges and needn't reach their ends.
Inputs may be any that keep to these rules, and one draw needn't show every extreme that they name: `reference_index`: the slots of index d of pair name acquisitions from 16 * (d - 1) to 16 * (d + 2) - 1 only, clipped to the stack; on every index some slot names the lower end of that range. `secondary_index`: each slot's secondary acquisition lies 1 to 3 after its reference acquisition and within the same range as the reference indices of that index of pair.
All inputs are finite; a program needn't handle non-finite values. No bound on the sum of `pair_count` on one device may be relied on, other than what follows from the above.
Results may differ from the reference program's by a relative error of at most 0.0003.
Values may be sent and summed in bfloat16 or wider, within the bound.
A program may use at most 64 MiB of HBM per device.

```python
import math
import jax
import jax.numpy as jnp
import numpy as np
from jax import lax

ACQ_DEV = 16
PAIR_DEV = 4
ACQ = 1024
PAIRS = 256
LINES = 40
SAMPLES = 5120
N_PAIR = 64


def pair_draw(key):
    base = jax.random.fold_in(key, 7)
    first_key, second_key = jax.random.split(base)
    slots = jnp.arange(PAIRS, dtype=jnp.int32)
    owner = slots // PAIR_DEV
    position = slots % PAIR_DEV
    lowest = jnp.maximum(ACQ_DEV * (owner - 1), 0)
    highest = jnp.minimum(ACQ_DEV * (owner + 2), ACQ)
    spread = highest - lowest - 1
    picked = jax.random.randint(first_key, (PAIRS,), 0, 1 << 20) % spread + lowest
    spacing = jax.random.randint(second_key, (PAIRS,), 1, 4)
    first_index = jnp.where(position == 0, lowest, jnp.where(position == 1, highest - 2, picked))
    second_index = jnp.minimum(first_index + spacing, highest - 1)
    second_index = jnp.where(position == 0, lowest + 1, second_index)
    second_index = jnp.where(position == 1, highest - 1, second_index)
    return (first_index.astype(jnp.int32), second_index.astype(jnp.int32))


def draw_reference_index(key, part):
    return pair_draw(key)[0]


def draw_secondary_index(key, part):
    return pair_draw(key)[1]


def draw_acquisitions(key, part):
    keys = jax.random.split(jax.random.fold_in(key, 11), 3)
    common = jax.random.normal(keys[0], (2, LINES, SAMPLES), jnp.float32)
    gains = jax.random.uniform(keys[1], (ACQ, 1, 1, 1), jnp.float32, 0.5, 1.5)
    noise = jax.random.normal(keys[2], (ACQ, 2, LINES, SAMPLES), jnp.float32) * 0.6
    field = common[None] * gains + noise
    return jnp.clip(field, -8.0, 8.0).astype(jnp.bfloat16)


def length_profile(number_of, total, most, skew):
    weights = [(1 << 20) // math.isqrt(grade ** skew) + 1 for grade in range(2, number_of + 1)]
    spare, counts = total - most - (number_of - 1), [1] * (number_of - 1)
    while spare > 0:
        free = [i for i in range(number_of - 1) if counts[i] < most]
        mass, budget = sum([weights[i] for i in free]), spare
        for i in free:
            more = min(most - counts[i], max(1, budget * weights[i] // mass), spare)
            counts[i] = counts[i] + more
            spare = spare - more
    return np.array([most] + counts)


def uneven(rng, amount, total, bound, lean):
    if amount == 2:
        one = jax.random.randint(rng, (), max(1, total - bound), min(bound, total - 1) + 1)
        return jnp.stack([one, total - one])
    lengths = jnp.asarray(length_profile(amount, total, bound, lean), jnp.int32)
    couples = (amount - 1) // 2
    donor, sink = lengths[1:1 + 2 * couples:2], lengths[2:2 + 2 * couples:2]
    room = jnp.minimum(donor - 1, bound - sink)
    shifted = jax.random.randint(jax.random.fold_in(rng, 1), (couples,), 0, 1 << 20) % (room + 1)
    lengths = lengths.at[1:1 + 2 * couples:2].set(donor - shifted).at[2:2 + 2 * couples:2].set(sink + shifted)
    return lengths[jax.random.permutation(jax.random.fold_in(rng, 2), amount)]


def setup_inputs(seed: int = 0) -> dict:
    arg_keys = jax.random.split(jax.random.key(seed), 5)
    return {
        "acquisitions": draw_acquisitions(jax.random.fold_in(arg_keys[4], 71), 0),
        "reference_index": draw_reference_index(jax.random.fold_in(arg_keys[4], 71), 0),
        "secondary_index": draw_secondary_index(jax.random.fold_in(arg_keys[4], 71), 0),
        "pair_count": uneven(arg_keys[3], N_PAIR, N_PAIR * PAIR_DEV * 5 // 8, PAIR_DEV, 2).astype(jnp.int32),
    }


def window_sum(products):
    out_lines = (products.shape[-2] - 6) // 5
    out_cols = (products.shape[-1] - 22) // 20
    range_sums = products[..., 1:1 + 20 * out_cols:20]
    for offset in range(2, 42):
        range_sums = range_sums + products[..., offset:offset + 20 * out_cols:20]
    line_sums = range_sums[..., 0:5 * out_lines:5, :]
    for offset in range(1, 11):
        line_sums = line_sums + range_sums[..., offset:offset + 5 * out_lines:5, :]
    return line_sums

def pair_outputs(first_slab, second_slab):
    first_real = first_slab[0].astype(jnp.float32)
    first_imag = first_slab[1].astype(jnp.float32)
    second_real = second_slab[0].astype(jnp.float32)
    second_imag = second_slab[1].astype(jnp.float32)
    stacked = jnp.stack([first_real * second_real + first_imag * second_imag, first_imag * second_real - first_real * second_imag, first_real * first_real + first_imag * first_imag, second_real * second_real + second_imag * second_imag])
    window_sums = window_sum(stacked)
    interferogram = window_sums[0:2] / 451.0
    coherence = jnp.sqrt(window_sums[0] * window_sums[0] + window_sums[1] * window_sums[1]) / jnp.sqrt(window_sums[2] * window_sums[3] + 1e-06)
    return (interferogram, coherence)

def reference(acquisitions, reference_index, secondary_index, pair_count):
    padded = jnp.pad(acquisitions, ((0, 0), (0, 0), (3, 3), (11, 11)))

    def one_pair(indices):
        first_slab = lax.dynamic_index_in_dim(padded, indices[0].astype(jnp.int32), 0, keepdims=False)
        second_slab = lax.dynamic_index_in_dim(padded, indices[1].astype(jnp.int32), 0, keepdims=False)
        return pair_outputs(first_slab, second_slab)
    interferogram, coherence = lax.map(one_pair, (reference_index, secondary_index))
    slots = jnp.arange(PAIRS, dtype=jnp.int32)
    live_slots = slots % PAIR_DEV < pair_count[slots // PAIR_DEV]
    interferogram = jnp.where(live_slots[:, None, None, None], interferogram, jnp.float32(0.0))
    coherence = jnp.where(live_slots[:, None, None], coherence, jnp.float32(0.0))
    return (interferogram, coherence)
```

```python
import jax
import jax.numpy as jnp
from jax import lax
from jax.experimental import pallas as pl
from jax.experimental.layout import Layout, with_layout_constraint
from jax.experimental.pallas import tpu as pltpu
from jax.sharding import PartitionSpec as P

MESH = pl.DeviceIdType.MESH
ACQ = 16
SLOTS = 4
LINES = 20
TILES = 20
WIDE = TILES + 1
EDGE = 3
COMBOS = ((13, 0), (14, 0), (15, 0), (14, 1), (15, 1), (15, 2))
CROSS = 2 * 3 * SLOTS
EARLY = CROSS + ACQ
LATE = 2 * len(COMBOS)
PITCH = 24
ROWS = LINES * WIDE * 2
F32 = jnp.float32
BF16 = jnp.bfloat16


def kernel(
    acq, ref_hbm, sec_hbm, cnt_hbm, ifg, coh,
    block, edge, relay_a, relay_b, wide, wide_edge, table,
    sums, lhs, early, late,
    out_a, out_b, in_a, in_b,
    ref_own, sec_own, ref_prev, sec_prev, ref_next, sec_next, count,
    local_sem, slab_send, relay_recv, pass_send, edge_recv,
    tile_send, tile_recv, index_send, index_recv, back_send, back_recv,
):
    d = lax.axis_index("pair")
    az = lax.axis_index("az")
    rg = lax.axis_index("rg")
    n = lax.axis_size("pair")
    oaz = 1 - az
    org = 1 - rg

    def at(step):
        return lax.rem(d + step + n, n)

    prev, nxt = at(-1), at(1)
    twin = d + 1 - 2 * lax.rem(d, 2)
    first = base = ACQ * d
    upper = az == 0

    own = [
        pltpu.make_async_copy(acq, block.at[:, :, pl.ds(0, TILES)], local_sem.at[0]),
        pltpu.make_async_copy(ref_hbm, ref_own, local_sem.at[1]),
        pltpu.make_async_copy(sec_hbm, sec_own, local_sem.at[2]),
        pltpu.make_async_copy(cnt_hbm, count, local_sem.at[3]),
    ]
    for copy in own:
        copy.start()

    barrier = pltpu.get_barrier_semaphore()
    peers = [
        (d, az, org), (d, oaz, rg),
        (prev, az, rg), (nxt, az, rg),
        (prev, az, org), (nxt, az, org),
        (prev, oaz, rg), (nxt, oaz, rg),
        (at(-2), oaz, rg), (at(2), oaz, rg),
    ]
    for peer in peers:
        pl.semaphore_signal(barrier, inc=1, device_id=peer, device_id_type=MESH)

    col = lax.broadcasted_iota(jnp.int32, (128, 128), 1) * 20
    row = lax.broadcasted_iota(jnp.int32, (128, 128), 0)
    for t in range(WIDE):
        sample = row + 128 * t
        if t == TILES:
            sample = sample - (128 * WIDE) * rg
        inside = (sample >= col - 10) & (sample <= col + 30)
        table[pl.ds(128 * t, 128), :] = jnp.where(inside, 1.0, 0.0).astype(BF16)

    pl.semaphore_wait(barrier, len(peers))

    def remote(src, dst, send, recv, device):
        return pltpu.make_async_remote_copy(
            src_ref=src, dst_ref=dst, send_sem=send, recv_sem=recv,
            device_id=device, device_id_type=MESH,
        )

    half = LINES // 2
    slabs = []
    for a in range(EDGE):
        slabs.append((
            remote(acq.at[a, pl.ds(0, half)], relay_a.at[a],
                   slab_send.at[a, 0], relay_recv.at[a, 0], (d, oaz, rg)),
            remote(acq.at[a, pl.ds(half, half)], relay_b.at[a],
                   slab_send.at[a, 1], relay_recv.at[a, 1], (twin, oaz, rg)),
        ))
    border = (TILES - 1) * org
    tiles = [
        remote(acq.at[:, :, border], block.at[:, :, TILES],
               tile_send.at[0], tile_recv.at[0], (d, az, org)),
        remote(acq.at[pl.ds(0, EDGE), :, border], edge.at[:, :, TILES],
               tile_send.at[1], tile_recv.at[1], (prev, az, org)),
    ]
    indices = [
        remote(ref_hbm, ref_next, index_send.at[0], index_recv.at[0], (prev, az, rg)),
        remote(sec_hbm, sec_next, index_send.at[1], index_recv.at[1], (prev, az, rg)),
        remote(ref_hbm, ref_prev, index_send.at[2], index_recv.at[2], (nxt, az, rg)),
        remote(sec_hbm, sec_prev, index_send.at[3], index_recv.at[3], (nxt, az, rg)),
    ]
    tiles[0].start()
    for copy in indices:
        copy.start()
    for pair in slabs:
        for copy in pair:
            copy.start()
    tiles[1].start()

    passes = []
    twin_prev = lax.rem(twin - 1 + n, n)
    for a in range(EDGE):
        passes.append((
            remote(relay_a.at[a], edge.at[a, pl.ds(0, half), pl.ds(0, TILES)],
                   pass_send.at[a, 0], edge_recv.at[a, 0], (prev, oaz, rg)),
            remote(relay_b.at[a], edge.at[a, pl.ds(half, half), pl.ds(0, TILES)],
                   pass_send.at[a, 1], edge_recv.at[a, 1], (twin_prev, oaz, rg)),
        ))

    def relay(a):
        for h in range(2):
            slabs[a][h].wait_recv()
            passes[a][h].start()

    def line(ref, a, l):
        start = a * ROWS + l * (2 * WIDE)
        return (
            ref[pl.ds(start, WIDE, stride=2), :],
            ref[pl.ds(start + 1, WIDE, stride=2), :],
        )

    def put(plane, window, value):
        start = pl.multiple_of((plane * 8 + window) * PITCH, 8)
        sums[pl.ds(start, WIDE), :] = value

    def line_sums(plane, get):
        def add(*terms):
            total = terms[0]
            for term in terms[1:]:
                total = tuple(x + y for x, y in zip(total, term))
            return total

        def store(window, value):
            for i, v in enumerate(value):
                put(plane + i, window, v)

        l2 = None
        s0 = add(get(0), get(1))
        l2 = get(2)
        up = add(s0, l2)
        s3 = add(get(3), get(4), get(5), get(6))
        l7 = get(7)
        m1 = add(s3, l7)
        store(0, add(up, m1))
        s8 = add(get(8), get(9), get(10), get(11))
        l12 = get(12)
        m2 = add(s8, l12)
        store(1, add(l2, m1, m2))
        s13 = add(get(13), get(14), get(15), get(16))
        l17 = get(17)
        m3 = add(s13, l17)
        store(2, add(l7, m2, m3))
        down = add(l17, get(18), get(19))
        store(3, add(l12, s13, down))
        store(4, tuple(jnp.where(upper, x, y) for x, y in zip(down, up)))

    def power(plane, a):
        def get(l):
            x, y = line(wide, a, l)
            return (x * x + y * y,)
        line_sums(plane, get)

    def cross(plane, a, other, b):
        def get(l):
            xr, yr = line(wide, a, l)
            xs, ys = line(other, b, l)
            return (xr * xs + yr * ys, yr * xs - xr * ys)
        line_sums(plane, get)

    def range_sums(planes, result):
        rows = planes * 8
        for t in range(WIDE):
            v = sums[pl.ds(t, rows, stride=PITCH), :]
            hi = v.astype(BF16)
            lo = (v - hi.astype(F32)).astype(BF16)
            lhs[pl.ds(0, rows), pl.ds(128 * t, 128)] = hi
            lhs[pl.ds(rows, rows), pl.ds(128 * t, 128)] = lo
        both = jnp.dot(lhs[pl.ds(0, 2 * rows), :], table[...], preferred_element_type=F32)
        total = both[:rows] + both[rows:]
        result[...] = total.reshape(planes, 8, 128)

    own[0].wait()
    tiles[0].wait_recv()

    def widen(a, carry):
        start = pl.multiple_of(a * ROWS, 8)
        wide[pl.ds(start, ROWS), :] = block[a].reshape(ROWS, 128).astype(F32)
        return carry

    lax.fori_loop(0, ACQ, widen, 0)

    def power_step(a, carry):
        power(CROSS + a, a)
        return carry

    lax.fori_loop(0, ACQ, power_step, 0)
    relay(0)

    for copy in own[1:]:
        copy.wait()
    for copy in indices:
        copy.wait_recv()
    names = [(ref_prev, sec_prev), (ref_own, sec_own), (ref_next, sec_next)]

    def clip(i):
        return jnp.clip(i, 0, ACQ - 1)

    for g, (refs, secs) in enumerate(names):
        def cross_step(k, carry, g=g, refs=refs, secs=secs):
            cross(2 * (SLOTS * g + k), clip(refs[k] - base), wide, clip(secs[k] - base))
            return carry
        lax.fori_loop(0, SLOTS, cross_step, 0)
        if g == 1:
            relay(1)

    range_sums(EARLY, early)
    relay(2)

    tiles[1].wait_recv()
    done = 0
    for a in range(EDGE):
        for h in range(2):
            passes[a][h].wait_recv()
        wide_edge[pl.ds(a * ROWS, ROWS), :] = edge[a].reshape(ROWS, 128).astype(F32)
        for i, (r, s) in enumerate(COMBOS):
            if s == a:
                cross(2 * i, r, wide_edge, s)
    range_sums(LATE, late)

    zero = jnp.zeros((8, 128), F32)
    for g, (refs, secs) in enumerate(names):
        for k in range(SLOTS):
            r = refs[k] - base
            s = secs[k] - base
            has_r = (r >= 0) & (r < ACQ)
            has_s = (s >= 0) & (s < ACQ)
            inner = has_r & (s < ACQ)
            outer = has_r & (s >= ACQ)
            combo = jnp.where(s == ACQ, r - 13, jnp.where(s == ACQ + 1, r - 11, 5))
            combo = jnp.clip(combo, 0, len(COMBOS) - 1)
            for c in range(4):
                if c < 2:
                    value = jnp.where(inner, early[2 * (SLOTS * g + k) + c], zero)
                    if g > 0:
                        value = value + jnp.where(outer, late[2 * combo + c], zero)
                elif c == 2:
                    value = jnp.where(has_r, early[CROSS + clip(r)], zero)
                else:
                    value = jnp.where(has_s, early[CROSS + clip(s)], zero)
                out_a[g, 4 * k + c] = value[0:4]
                out_b[g, pl.ds(4 * k + c, 1), :] = value[4:5]

    backs = [
        remote(out_b.at[1], in_b.at[1], back_send.at[3], back_recv.at[3], (d, oaz, rg)),
        remote(out_a.at[0], in_a.at[1], back_send.at[0], back_recv.at[0], (prev, az, rg)),
        remote(out_a.at[2], in_a.at[0], back_send.at[1], back_recv.at[1], (nxt, az, rg)),
        remote(out_b.at[0], in_b.at[2], back_send.at[2], back_recv.at[2], (prev, oaz, rg)),
        remote(out_b.at[2], in_b.at[0], back_send.at[4], back_recv.at[4], (nxt, oaz, rg)),
    ]
    for copy in backs:
        copy.start()
    for copy in tiles + indices:
        copy.wait_send()
    for a in range(EDGE):
        for h in range(2):
            slabs[a][h].wait_send()
            passes[a][h].wait_send()
    for copy in backs:
        copy.wait()

    window = lax.broadcasted_iota(jnp.int32, (4, 128), 0)
    shared = window == 3 * oaz
    for k in range(SLOTS):
        live = k < count[0]
        total = []
        for c in range(4):
            i = 4 * k + c
            rim = in_b[0, pl.ds(i, 1), :] + in_b[1, pl.ds(i, 1), :] + in_b[2, pl.ds(i, 1), :]
            body = out_a[1, i] + in_a[0, i] + in_a[1, i]
            total.append(body + jnp.where(shared, rim, 0.0))
        re, im, pr, ps = total
        none = jnp.zeros((4, 128), F32)
        ifg[k, 0] = jnp.where(live, re / 451.0, none)
        ifg[k, 1] = jnp.where(live, im / 451.0, none)
        value = jnp.sqrt(re * re + im * im) / jnp.sqrt(pr * ps + 1e-06)
        coh[k] = jnp.where(live, value, none)


def on_device(acquisitions, reference_index, secondary_index, pair_count):
    view = acquisitions.reshape(ACQ, 2, LINES, TILES, 128)
    view = with_layout_constraint(view, Layout((0, 2, 3, 1, 4)))
    view = view.transpose(0, 2, 3, 1, 4)
    hbm = pl.BlockSpec(memory_space=pl.ANY)
    vmem = pl.BlockSpec(memory_space=pltpu.VMEM)
    dma = pltpu.SemaphoreType.DMA
    return pl.pallas_call(
        kernel,
        out_shape=(
            jax.ShapeDtypeStruct((SLOTS, 2, 4, 128), F32),
            jax.ShapeDtypeStruct((SLOTS, 4, 128), F32),
        ),
        in_specs=[hbm] * 4,
        out_specs=(vmem, vmem),
        scratch_shapes=[
            pltpu.VMEM((ACQ, LINES, WIDE, 2, 128), BF16),
            pltpu.VMEM((EDGE, LINES, WIDE, 2, 128), BF16),
            pltpu.VMEM((EDGE, LINES // 2, TILES, 2, 128), BF16),
            pltpu.VMEM((EDGE, LINES // 2, TILES, 2, 128), BF16),
            pltpu.VMEM((ACQ * ROWS, 128), F32),
            pltpu.VMEM((EDGE * ROWS, 128), F32),
            pltpu.VMEM((128 * WIDE, 128), BF16),
            pltpu.VMEM((EARLY * 8 * PITCH, 128), F32),
            pltpu.VMEM((EARLY * 16, 128 * WIDE), BF16),
            pltpu.VMEM((EARLY, 8, 128), F32),
            pltpu.VMEM((LATE, 8, 128), F32),
            pltpu.VMEM((3, 16, 4, 128), F32),
            pltpu.VMEM((3, 16, 128), F32),
            pltpu.VMEM((2, 16, 4, 128), F32),
            pltpu.VMEM((3, 16, 128), F32),
        ] + [pltpu.SMEM((SLOTS,), jnp.int32)] * 6 + [pltpu.SMEM((1,), jnp.int32)] + [
            dma((4,)), dma((EDGE, 2)), dma((EDGE, 2)), dma((EDGE, 2)), dma((EDGE, 2)),
            dma((2,)), dma((2,)), dma((4,)), dma((4,)), dma((5,)), dma((5,)),
        ],
        compiler_params=pltpu.CompilerParams(
            collective_id=0, has_side_effects=True, vmem_limit_bytes=60 * 2**20
        ),
    )(view, reference_index, secondary_index, pair_count)


def solution(mesh):
    return jax.shard_map(
        on_device,
        mesh=mesh,
        in_specs=(P("pair", None, "az", "rg"), P("pair"), P("pair"), P("pair")),
        out_specs=(P("pair", None, "az", "rg"), P("pair", "az", "rg")),
        check_vma=False,
    )
```

```python
import jax
import jax.numpy as jnp
from jax import lax
from jax.experimental import pallas as pl
from jax.experimental.layout import Layout, with_layout_constraint
from jax.experimental.pallas import tpu as pltpu
from jax.sharding import PartitionSpec as P

MESH = pl.DeviceIdType.MESH
ACQ = 16
SLOTS = 4
LINES = 20
TILES = 20
WIDE = TILES + 1
EDGE = 3
COMBOS = ((2, 0), (2, 1), (2, 2), (1, 0), (1, 1), (0, 0))
CROSS = 2 * 3 * SLOTS
EARLY = CROSS + ACQ
LATE = 2 * len(COMBOS)
PITCH = 24
ROWS = LINES * WIDE * 2
F32 = jnp.float32
BF16 = jnp.bfloat16


def kernel(
    acq, ref_hbm, sec_hbm, cnt_hbm, totals,
    block, edge, wide, wide_edge, table,
    sums, lhs, early, late,
    out_a, out_b, in_a, in_b, late_a, late_b, in_late_a, in_late_b,
    ref_own, sec_own, ref_prev, sec_prev, ref_next, sec_next, count,
    local_sem, slab_send, slab_recv,
    tile_send, tile_recv, index_send, index_recv, back_send, back_recv, late_send, late_recv,
):
    d = lax.axis_index("pair")
    az = lax.axis_index("az")
    rg = lax.axis_index("rg")
    n = lax.axis_size("pair")
    oaz = 1 - az
    org = 1 - rg

    def at(step):
        return lax.rem(d + step + n, n)

    prev, nxt = at(-1), at(1)
    base = ACQ * d
    upper = az == 0

    own = [
        pltpu.make_async_copy(acq, block.at[:, :, pl.ds(0, TILES)], local_sem.at[0]),
        pltpu.make_async_copy(ref_hbm, ref_own, local_sem.at[1]),
        pltpu.make_async_copy(sec_hbm, sec_own, local_sem.at[2]),
        pltpu.make_async_copy(cnt_hbm, count, local_sem.at[3]),
    ]
    for copy in own:
        copy.start()

    barrier = pltpu.get_barrier_semaphore()
    peers = [
        (d, az, org), (d, oaz, rg),
        (prev, az, rg), (nxt, az, rg),
        (prev, az, org), (nxt, az, org),
        (prev, oaz, rg), (nxt, oaz, rg),
    ]
    for peer in peers:
        pl.semaphore_signal(barrier, inc=1, device_id=peer, device_id_type=MESH)

    col = lax.broadcasted_iota(jnp.int32, (128, 128), 1) * 20
    row = lax.broadcasted_iota(jnp.int32, (128, 128), 0)
    for t in range(WIDE):
        sample = row + 128 * t
        if t == TILES:
            sample = sample - (128 * WIDE) * rg
        inside = (sample >= col - 10) & (sample <= col + 30)
        table[pl.ds(128 * t, 128), :] = jnp.where(inside, 1.0, 0.0).astype(BF16)

    pl.semaphore_wait(barrier, len(peers))

    def remote(src, dst, send, recv, device):
        return pltpu.make_async_remote_copy(
            src_ref=src, dst_ref=dst, send_sem=send, recv_sem=recv,
            device_id=device, device_id_type=MESH,
        )

    slabs = [
        remote(acq.at[ACQ - EDGE + a], edge.at[a, :, pl.ds(0, TILES)],
               slab_send.at[a], slab_recv.at[a], (nxt, az, rg))
        for a in range(EDGE)
    ]
    border = (TILES - 1) * org
    tiles = [
        remote(acq.at[:, :, border], block.at[:, :, TILES],
               tile_send.at[0], tile_recv.at[0], (d, az, org)),
        remote(acq.at[pl.ds(ACQ - EDGE, EDGE), :, border], edge.at[:, :, TILES],
               tile_send.at[1], tile_recv.at[1], (nxt, az, org)),
    ]
    indices = [
        remote(ref_hbm, ref_next, index_send.at[0], index_recv.at[0], (prev, az, rg)),
        remote(sec_hbm, sec_next, index_send.at[1], index_recv.at[1], (prev, az, rg)),
        remote(ref_hbm, ref_prev, index_send.at[2], index_recv.at[2], (nxt, az, rg)),
        remote(sec_hbm, sec_prev, index_send.at[3], index_recv.at[3], (nxt, az, rg)),
    ]
    for copy in indices:
        copy.start()
    for copy in tiles:
        copy.start()
    for a in (2, 1, 0):
        slabs[a].start()

    def line(ref, a, l):
        start = a * ROWS + l * (2 * WIDE)
        return (
            ref[pl.ds(start, WIDE, stride=2), :],
            ref[pl.ds(start + 1, WIDE, stride=2), :],
        )

    def put(plane, window, value):
        start = pl.multiple_of((plane * 8 + window) * PITCH, 8)
        sums[pl.ds(start, WIDE), :] = value

    def line_sums(plane, get):
        def add(*terms):
            total = terms[0]
            for term in terms[1:]:
                total = tuple(x + y for x, y in zip(total, term))
            return total

        def store(window, value):
            for i, v in enumerate(value):
                put(plane + i, window, v)

        l2 = None
        s0 = add(get(0), get(1))
        l2 = get(2)
        up = add(s0, l2)
        s3 = add(get(3), get(4), get(5), get(6))
        l7 = get(7)
        m1 = add(s3, l7)
        store(0, add(up, m1))
        s8 = add(get(8), get(9), get(10), get(11))
        l12 = get(12)
        m2 = add(s8, l12)
        store(1, add(l2, m1, m2))
        s13 = add(get(13), get(14), get(15), get(16))
        l17 = get(17)
        m3 = add(s13, l17)
        store(2, add(l7, m2, m3))
        down = add(l17, get(18), get(19))
        store(3, add(l12, s13, down))
        store(4, tuple(jnp.where(upper, x, y) for x, y in zip(down, up)))

    def power(plane, a):
        def get(l):
            x, y = line(wide, a, l)
            return (x * x + y * y,)
        line_sums(plane, get)

    def cross(plane, one, a, b):
        def get(l):
            xr, yr = line(one, a, l)
            xs, ys = line(wide, b, l)
            return (xr * xs + yr * ys, yr * xs - xr * ys)
        line_sums(plane, get)

    def range_sums(first, planes, result):
        rows = planes * 8
        for t in range(WIDE):
            v = sums[pl.ds(first * 8 * PITCH + t, rows, stride=PITCH), :]
            hi = v.astype(BF16)
            lo = (v - hi.astype(F32)).astype(BF16)
            lhs[pl.ds(0, rows), pl.ds(128 * t, 128)] = hi
            lhs[pl.ds(rows, rows), pl.ds(128 * t, 128)] = lo
        both = jnp.dot(lhs[pl.ds(0, 2 * rows), :], table[...], preferred_element_type=F32)
        total = both[:rows] + both[rows:]
        result[pl.ds(first, planes)] = total.reshape(planes, 8, 128)

    own[0].wait()
    tiles[0].wait_recv()

    def widen(a, carry):
        start = pl.multiple_of(a * ROWS, 8)
        wide[pl.ds(start, ROWS), :] = block[a].reshape(ROWS, 128).astype(F32)
        return carry

    lax.fori_loop(0, ACQ, widen, 0)

    def power_step(a, carry):
        power(CROSS + a, a)
        return carry

    lax.fori_loop(0, ACQ, power_step, 0)

    for copy in own[1:]:
        copy.wait()
    for copy in indices:
        copy.wait_recv()
    names = [(ref_prev, sec_prev), (ref_own, sec_own), (ref_next, sec_next)]

    def clip(i):
        return jnp.clip(i, 0, ACQ - 1)

    for g, (refs, secs) in enumerate(names):
        def cross_step(k, carry, g=g, refs=refs, secs=secs):
            cross(2 * (SLOTS * g + k), wide, clip(refs[k] - base), clip(secs[k] - base))
            return carry
        lax.fori_loop(0, SLOTS, cross_step, 0)

    range_sums(0, EARLY, early)

    zero = jnp.zeros((8, 128), F32)
    for g, (refs, secs) in enumerate(names):
        for k in range(SLOTS):
            r = refs[k] - base
            s = secs[k] - base
            has_r = (r >= 0) & (r < ACQ)
            has_s = (s >= 0) & (s < ACQ)
            for c in range(4):
                if c < 2:
                    value = jnp.where(has_r & has_s, early[2 * (SLOTS * g + k) + c], zero)
                elif c == 2:
                    value = jnp.where(has_r, early[CROSS + clip(r)], zero)
                else:
                    value = jnp.where(has_s, early[CROSS + clip(s)], zero)
                out_a[g, 4 * k + c] = value[0:4]
                out_b[g, pl.ds(4 * k + c, 1), :] = value[4:5]

    backs = [
        remote(out_a.at[2], in_a.at[0], back_send.at[1], back_recv.at[1], (nxt, az, rg)),
        remote(out_b.at[2], in_b.at[0], back_send.at[4], back_recv.at[4], (nxt, oaz, rg)),
        remote(out_a.at[0], in_a.at[1], back_send.at[0], back_recv.at[0], (prev, az, rg)),
        remote(out_b.at[0], in_b.at[2], back_send.at[2], back_recv.at[2], (prev, oaz, rg)),
        remote(out_b.at[1], in_b.at[1], back_send.at[3], back_recv.at[3], (d, oaz, rg)),
    ]
    for copy in backs:
        copy.start()

    tiles[1].wait_recv()
    for a in (2, 1, 0):
        slabs[a].wait_recv()
        wide_edge[pl.ds(a * ROWS, ROWS), :] = edge[a].reshape(ROWS, 128).astype(F32)
        for i, (r, s) in enumerate(COMBOS):
            if r == a:
                cross(2 * i, wide_edge, r, s)
        if a == 1:
            range_sums(0, 10, late)
    range_sums(10, 2, late)

    for g, (refs, secs) in enumerate(names[:2]):
        for k in range(SLOTS):
            r = refs[k] - base
            s = secs[k] - base
            reach = (r < 0) & (s >= 0) & (s < ACQ)
            combo = jnp.where(r == -1, s, jnp.where(r == -2, s + 3, 5))
            combo = jnp.clip(combo, 0, len(COMBOS) - 1)
            for c in range(2):
                value = jnp.where(reach, late[2 * combo + c], zero)
                late_a[g, 2 * k + c] = value[0:4]
                late_b[g, pl.ds(2 * k + c, 1), :] = value[4:5]

    lates = [
        remote(late_a.at[0], in_late_a, late_send.at[0], late_recv.at[0], (prev, az, rg)),
        remote(late_b.at[0], in_late_b.at[0], late_send.at[1], late_recv.at[1], (prev, oaz, rg)),
        remote(late_b.at[1], in_late_b.at[1], late_send.at[2], late_recv.at[2], (d, oaz, rg)),
    ]
    for copy in lates:
        copy.start()
    for copy in tiles + indices + slabs:
        copy.wait_send()
    for copy in backs + lates:
        copy.wait()

    window = lax.broadcasted_iota(jnp.int32, (4, 128), 0)
    shared = window == 3 * oaz
    for k in range(SLOTS):
        live = k < count[0]
        for c in range(4):
            i = 4 * k + c
            rim = in_b[0, pl.ds(i, 1), :] + in_b[1, pl.ds(i, 1), :] + in_b[2, pl.ds(i, 1), :]
            body = out_a[1, i] + in_a[0, i] + in_a[1, i]
            if c < 2:
                j = 2 * k + c
                rim = rim + in_late_b[0, pl.ds(j, 1), :] + in_late_b[1, pl.ds(j, 1), :]
                body = body + late_a[1, j] + in_late_a[j]
            total = body + jnp.where(shared, rim, 0.0)
            if c < 2:
                total = jnp.where(live, total, jnp.zeros((4, 128), F32))
            totals[k, c] = total


def finish(totals, ifg, coh):
    re, im = totals[:, 0], totals[:, 1]
    ifg[:, 0] = re / 451.0
    ifg[:, 1] = im / 451.0
    coh[...] = jnp.sqrt(re * re + im * im) / jnp.sqrt(totals[:, 2] * totals[:, 3] + 1e-06)


def on_device(acquisitions, reference_index, secondary_index, pair_count):
    view = acquisitions.reshape(ACQ, 2, LINES, TILES, 128)
    view = with_layout_constraint(view, Layout((0, 2, 3, 1, 4)))
    view = view.transpose(0, 2, 3, 1, 4)
    hbm = pl.BlockSpec(memory_space=pl.ANY)
    vmem = pl.BlockSpec(memory_space=pltpu.VMEM)
    dma = pltpu.SemaphoreType.DMA
    totals = pl.pallas_call(
        kernel,
        out_shape=jax.ShapeDtypeStruct((SLOTS, 4, 4, 128), F32),
        in_specs=[hbm] * 4,
        out_specs=vmem,
        scratch_shapes=[
            pltpu.VMEM((ACQ, LINES, WIDE, 2, 128), BF16),
            pltpu.VMEM((EDGE, LINES, WIDE, 2, 128), BF16),
            pltpu.VMEM((ACQ * ROWS, 128), F32),
            pltpu.VMEM((EDGE * ROWS, 128), F32),
            pltpu.VMEM((128 * WIDE, 128), BF16),
            pltpu.VMEM((EARLY * 8 * PITCH, 128), F32),
            pltpu.VMEM((EARLY * 16, 128 * WIDE), BF16),
            pltpu.VMEM((EARLY, 8, 128), F32),
            pltpu.VMEM((LATE, 8, 128), F32),
            pltpu.VMEM((3, 16, 4, 128), F32),
            pltpu.VMEM((3, 16, 128), F32),
            pltpu.VMEM((2, 16, 4, 128), F32),
            pltpu.VMEM((3, 16, 128), F32),
            pltpu.VMEM((2, 8, 4, 128), F32),
            pltpu.VMEM((2, 8, 128), F32),
            pltpu.VMEM((8, 4, 128), F32),
            pltpu.VMEM((2, 8, 128), F32),
        ] + [pltpu.SMEM((SLOTS,), jnp.int32)] * 6 + [pltpu.SMEM((1,), jnp.int32)] + [
            dma((4,)), dma((EDGE,)), dma((EDGE,)), dma((2,)), dma((2,)),
            dma((4,)), dma((4,)), dma((5,)), dma((5,)), dma((3,)), dma((3,)),
        ],
        compiler_params=pltpu.CompilerParams(
            collective_id=0, has_side_effects=True, vmem_limit_bytes=60 * 2**20
        ),
    )(view, reference_index, secondary_index, pair_count)
    return pl.pallas_call(
        finish,
        out_shape=(
            jax.ShapeDtypeStruct((SLOTS, 2, 4, 128), F32),
            jax.ShapeDtypeStruct((SLOTS, 4, 128), F32),
        ),
        in_specs=[vmem],
        out_specs=(vmem, vmem),
    )(totals)


def solution(mesh):
    return jax.shard_map(
        on_device,
        mesh=mesh,
        in_specs=(P("pair", None, "az", "rg"), P("pair"), P("pair"), P("pair")),
        out_specs=(P("pair", None, "az", "rg"), P("pair", "az", "rg")),
        check_vma=False,
    )
```

```python
import jax
import jax.numpy as jnp
from jax import lax
from jax.experimental import pallas as pl
from jax.experimental.layout import Layout, with_layout_constraint
from jax.experimental.pallas import tpu as pltpu
from jax.sharding import PartitionSpec as P

MESH = pl.DeviceIdType.MESH
ACQ = 16
SLOTS = 4
LINES = 20
TILES = 20
WIDE = TILES + 1
EDGE = 3
COMBOS = ((2, 0), (2, 1), (2, 2), (1, 0), (1, 1), (0, 0))
CROSS = 2 * 3 * SLOTS
EARLY = CROSS + ACQ
LATE = 2 * len(COMBOS)
PITCH = 24
ROWS = LINES * WIDE * 2
F32 = jnp.float32
BF16 = jnp.bfloat16


def kernel(
    acq, ref_hbm, sec_hbm, totals,
    block, edge, wide, wide_edge, table,
    sums, lhs, early, late,
    out_a, out_b, in_a, in_b, late_a, late_b, in_late_a, in_late_b,
    ref_own, sec_own, ref_prev, sec_prev, ref_next, sec_next,
    local_sem, slab_send, slab_recv,
    tile_send, tile_recv, index_send, index_recv, back_send, back_recv, late_send, late_recv, ready,
):
    d = lax.axis_index("pair")
    az = lax.axis_index("az")
    rg = lax.axis_index("rg")
    n = lax.axis_size("pair")
    oaz = 1 - az
    org = 1 - rg

    def at(step):
        return lax.rem(d + step + n, n)

    prev, nxt = at(-1), at(1)
    base = ACQ * d
    upper = az == 0

    own = [
        pltpu.make_async_copy(acq, block.at[:, :, pl.ds(0, TILES)], local_sem.at[0]),
        pltpu.make_async_copy(ref_hbm, ref_own, local_sem.at[1]),
        pltpu.make_async_copy(sec_hbm, sec_own, local_sem.at[2]),
    ]
    for copy in own:
        copy.start()

    barrier = pltpu.get_barrier_semaphore()
    peers = [
        (d, az, org), (d, oaz, rg),
        (prev, az, rg), (prev, az, org), (prev, oaz, rg),
    ]
    for peer in peers:
        pl.semaphore_signal(barrier, inc=1, device_id=peer, device_id_type=MESH)

    pl.semaphore_wait(barrier, len(peers))
    for peer in ((nxt, az, rg), (nxt, oaz, rg)):
        pl.semaphore_signal(ready, inc=1, device_id=peer, device_id_type=MESH)

    def remote(src, dst, send, recv, device):
        return pltpu.make_async_remote_copy(
            src_ref=src, dst_ref=dst, send_sem=send, recv_sem=recv,
            device_id=device, device_id_type=MESH,
        )

    slabs = [
        remote(acq.at[ACQ - EDGE + a], edge.at[a, :, pl.ds(0, TILES)],
               slab_send.at[a], slab_recv.at[a], (nxt, az, rg))
        for a in range(EDGE)
    ]
    border = (TILES - 1) * org
    tiles = [
        remote(acq.at[:, :, border], block.at[:, :, TILES],
               tile_send.at[0], tile_recv.at[0], (d, az, org)),
        remote(acq.at[pl.ds(ACQ - EDGE, EDGE), :, border], edge.at[:, :, TILES],
               tile_send.at[1], tile_recv.at[1], (nxt, az, org)),
    ]
    indices = [
        remote(ref_hbm, ref_next, index_send.at[0], index_recv.at[0], (prev, az, rg)),
        remote(sec_hbm, sec_next, index_send.at[1], index_recv.at[1], (prev, az, rg)),
        remote(ref_hbm, ref_prev, index_send.at[2], index_recv.at[2], (nxt, az, rg)),
        remote(sec_hbm, sec_prev, index_send.at[3], index_recv.at[3], (nxt, az, rg)),
    ]
    for copy in indices[2:]:
        copy.start()
    for copy in tiles:
        copy.start()
    for a in (2, 1, 0):
        slabs[a].start()

    col = lax.broadcasted_iota(jnp.int32, (128, 128), 1) * 20
    row = lax.broadcasted_iota(jnp.int32, (128, 128), 0)
    for t in range(WIDE):
        sample = row + 128 * t
        if t == TILES:
            sample = sample - (128 * WIDE) * rg
        inside = (sample >= col - 10) & (sample <= col + 30)
        table[pl.ds(128 * t, 128), :] = jnp.where(inside, 1.0, 0.0).astype(BF16)

    def line(ref, a, l):
        start = a * ROWS + l * (2 * WIDE)
        return (
            ref[pl.ds(start, WIDE, stride=2), :],
            ref[pl.ds(start + 1, WIDE, stride=2), :],
        )

    def put(plane, window, value):
        start = pl.multiple_of((plane * 8 + window) * PITCH, 8)
        sums[pl.ds(start, WIDE), :] = value

    def line_sums(plane, get):
        def add(*terms):
            total = terms[0]
            for term in terms[1:]:
                total = tuple(x + y for x, y in zip(total, term))
            return total

        def store(window, value):
            for i, v in enumerate(value):
                put(plane + i, window, v)

        l2 = None
        s0 = add(get(0), get(1))
        l2 = get(2)
        up = add(s0, l2)
        s3 = add(get(3), get(4), get(5), get(6))
        l7 = get(7)
        m1 = add(s3, l7)
        store(0, add(up, m1))
        s8 = add(get(8), get(9), get(10), get(11))
        l12 = get(12)
        m2 = add(s8, l12)
        store(1, add(l2, m1, m2))
        s13 = add(get(13), get(14), get(15), get(16))
        l17 = get(17)
        m3 = add(s13, l17)
        store(2, add(l7, m2, m3))
        down = add(l17, get(18), get(19))
        store(3, add(l12, s13, down))
        store(4, tuple(jnp.where(upper, x, y) for x, y in zip(down, up)))

    def power(plane, a):
        def get(l):
            x, y = line(wide, a, l)
            return (x * x + y * y,)
        line_sums(plane, get)

    def cross(plane, one, a, b):
        def get(l):
            xr, yr = line(one, a, l)
            xs, ys = line(wide, b, l)
            return (xr * xs + yr * ys, yr * xs - xr * ys)
        line_sums(plane, get)

    def range_sums(first, planes, result):
        rows = planes * 8
        for t in range(WIDE):
            v = sums[pl.ds(first * 8 * PITCH + t, rows, stride=PITCH), :]
            hi = v.astype(BF16)
            lo = (v - hi.astype(F32)).astype(BF16)
            lhs[pl.ds(0, rows), pl.ds(128 * t, 128)] = hi
            lhs[pl.ds(rows, rows), pl.ds(128 * t, 128)] = lo
        both = jnp.dot(lhs[pl.ds(0, 2 * rows), :], table[...], preferred_element_type=F32)
        total = both[:rows] + both[rows:]
        result[pl.ds(first, planes)] = total.reshape(planes, 8, 128)

    own[0].wait()
    tiles[0].wait_recv()

    def widen(a, carry):
        start = pl.multiple_of(a * ROWS, 8)
        wide[pl.ds(start, ROWS), :] = block[a].reshape(ROWS, 128).astype(F32)
        return carry

    lax.fori_loop(0, ACQ, widen, 0)

    def power_step(a, carry):
        power(CROSS + a, a)
        return carry

    lax.fori_loop(0, ACQ, power_step, 0)

    for copy in own[1:]:
        copy.wait()
    names = [(ref_prev, sec_prev), (ref_own, sec_own), (ref_next, sec_next)]

    def clip(i):
        return jnp.clip(i, 0, ACQ - 1)

    def group(g):
        refs, secs = names[g]

        def cross_step(k, carry):
            cross(2 * (SLOTS * g + k), wide, clip(refs[k] - base), clip(secs[k] - base))
            return carry

        lax.fori_loop(0, SLOTS, cross_step, 0)

    group(1)
    pl.semaphore_wait(ready, 2)
    for copy in indices[:2]:
        copy.start()
    for copy in indices[2:]:
        copy.wait_recv()
    group(0)
    for copy in indices[:2]:
        copy.wait_recv()
    group(2)

    range_sums(0, EARLY, early)

    zero = jnp.zeros((8, 128), F32)
    for g, (refs, secs) in enumerate(names):
        for k in range(SLOTS):
            r = refs[k] - base
            s = secs[k] - base
            has_r = (r >= 0) & (r < ACQ)
            has_s = (s >= 0) & (s < ACQ)
            for c in range(4):
                if c < 2:
                    value = jnp.where(has_r & has_s, early[2 * (SLOTS * g + k) + c], zero)
                elif c == 2:
                    value = jnp.where(has_r, early[CROSS + clip(r)], zero)
                else:
                    value = jnp.where(has_s, early[CROSS + clip(s)], zero)
                out_a[g, 4 * k + c] = value[0:4]
                out_b[g, pl.ds(4 * k + c, 1), :] = value[4:5]

    backs = [
        remote(out_a.at[2], in_a.at[0], back_send.at[1], back_recv.at[1], (nxt, az, rg)),
        remote(out_b.at[2], in_b.at[0], back_send.at[4], back_recv.at[4], (nxt, oaz, rg)),
        remote(out_a.at[0], in_a.at[1], back_send.at[0], back_recv.at[0], (prev, az, rg)),
        remote(out_b.at[0], in_b.at[2], back_send.at[2], back_recv.at[2], (prev, oaz, rg)),
        remote(out_b.at[1], in_b.at[1], back_send.at[3], back_recv.at[3], (d, oaz, rg)),
    ]
    for copy in backs:
        copy.start()

    tiles[1].wait_recv()
    for a in (2, 1, 0):
        slabs[a].wait_recv()
        wide_edge[pl.ds(a * ROWS, ROWS), :] = edge[a].reshape(ROWS, 128).astype(F32)
        for i, (r, s) in enumerate(COMBOS):
            if r == a:
                cross(2 * i, wide_edge, r, s)
        if a == 1:
            range_sums(0, 10, late)
    range_sums(10, 2, late)

    for g, (refs, secs) in enumerate(names[:2]):
        for k in range(SLOTS):
            r = refs[k] - base
            s = secs[k] - base
            reach = (r < 0) & (s >= 0) & (s < ACQ)
            combo = jnp.where(r == -1, s, jnp.where(r == -2, s + 3, 5))
            combo = jnp.clip(combo, 0, len(COMBOS) - 1)
            for c in range(2):
                value = jnp.where(reach, late[2 * combo + c], zero)
                late_a[g, 2 * k + c] = value[0:4]
                late_b[g, pl.ds(2 * k + c, 1), :] = value[4:5]

    lates = [
        remote(late_a.at[0], in_late_a, late_send.at[0], late_recv.at[0], (prev, az, rg)),
        remote(late_b.at[0], in_late_b.at[0], late_send.at[1], late_recv.at[1], (prev, oaz, rg)),
        remote(late_b.at[1], in_late_b.at[1], late_send.at[2], late_recv.at[2], (d, oaz, rg)),
    ]
    for copy in lates:
        copy.start()
    for copy in tiles + indices + slabs:
        copy.wait_send()
    for copy in backs + lates:
        copy.wait()

    window = lax.broadcasted_iota(jnp.int32, (4, 128), 0)
    shared = window == 3 * oaz
    for k in range(SLOTS):
        for c in range(4):
            i = 4 * k + c
            rim = in_b[0, pl.ds(i, 1), :] + in_b[1, pl.ds(i, 1), :] + in_b[2, pl.ds(i, 1), :]
            body = out_a[1, i] + in_a[0, i] + in_a[1, i]
            if c < 2:
                j = 2 * k + c
                rim = rim + in_late_b[0, pl.ds(j, 1), :] + in_late_b[1, pl.ds(j, 1), :]
                body = body + late_a[1, j] + in_late_a[j]
            totals[k, c] = body + jnp.where(shared, rim, 0.0)


def finish(totals, count, ifg, coh):
    slot = lax.broadcasted_iota(jnp.int32, (SLOTS, 4, 128), 0)
    live = slot < count[...].reshape(1, 1, 1)
    re, im = totals[:, 0], totals[:, 1]
    value = jnp.sqrt(re * re + im * im) / jnp.sqrt(totals[:, 2] * totals[:, 3] + 1e-06)
    ifg[:, 0] = jnp.where(live, re / 451.0, 0.0)
    ifg[:, 1] = jnp.where(live, im / 451.0, 0.0)
    coh[...] = jnp.where(live, value, 0.0)


def on_device(acquisitions, reference_index, secondary_index, pair_count):
    view = acquisitions.reshape(ACQ, 2, LINES, TILES, 128)
    view = with_layout_constraint(view, Layout((0, 2, 3, 1, 4)))
    view = view.transpose(0, 2, 3, 1, 4)
    hbm = pl.BlockSpec(memory_space=pltpu.HBM)
    vmem = pl.BlockSpec(memory_space=pltpu.VMEM)
    dma = pltpu.SemaphoreType.DMA
    totals = pl.pallas_call(
        kernel,
        out_shape=pltpu.VMEM((SLOTS, 4, 4, 128), F32),
        in_specs=[hbm] * 3,
        out_specs=vmem,
        scratch_shapes=[
            pltpu.VMEM((ACQ, LINES, WIDE, 2, 128), BF16),
            pltpu.VMEM((EDGE, LINES, WIDE, 2, 128), BF16),
            pltpu.VMEM((ACQ * ROWS, 128), F32),
            pltpu.VMEM((EDGE * ROWS, 128), F32),
            pltpu.VMEM((128 * WIDE, 128), BF16),
            pltpu.VMEM((EARLY * 8 * PITCH, 128), F32),
            pltpu.VMEM((EARLY * 16, 128 * WIDE), BF16),
            pltpu.VMEM((EARLY, 8, 128), F32),
            pltpu.VMEM((LATE, 8, 128), F32),
            pltpu.VMEM((3, 16, 4, 128), F32),
            pltpu.VMEM((3, 16, 128), F32),
            pltpu.VMEM((2, 16, 4, 128), F32),
            pltpu.VMEM((3, 16, 128), F32),
            pltpu.VMEM((2, 8, 4, 128), F32),
            pltpu.VMEM((2, 8, 128), F32),
            pltpu.VMEM((8, 4, 128), F32),
            pltpu.VMEM((2, 8, 128), F32),
        ] + [pltpu.SMEM((SLOTS,), jnp.int32)] * 6 + [
            dma((3,)), dma((EDGE,)), dma((EDGE,)), dma((2,)), dma((2,)),
            dma((4,)), dma((4,)), dma((5,)), dma((5,)), dma((3,)), dma((3,)),
            pltpu.SemaphoreType.REGULAR,
        ],
        compiler_params=pltpu.CompilerParams(
            collective_id=0, has_side_effects=True, vmem_limit_bytes=60 * 2**20
        ),
    )(view, reference_index, secondary_index)
    return pl.pallas_call(
        finish,
        out_shape=(
            jax.ShapeDtypeStruct((SLOTS, 2, 4, 128), F32),
            jax.ShapeDtypeStruct((SLOTS, 4, 128), F32),
        ),
        in_specs=[vmem, vmem],
        out_specs=(vmem, vmem),
        compiler_params=pltpu.CompilerParams(vmem_limit_bytes=2**20),
    )(totals, pair_count.reshape(1, 1))


def solution(mesh):
    return jax.shard_map(
        on_device,
        mesh=mesh,
        in_specs=(P("pair", None, "az", "rg"), P("pair"), P("pair"), P("pair")),
        out_specs=(P("pair", None, "az", "rg"), P("pair", "az", "rg")),
        check_vma=False,
    )
```

```python
import jax
import jax.numpy as jnp
from jax import lax
from jax.experimental import pallas as pl
from jax.experimental.layout import Layout, with_layout_constraint
from jax.experimental.pallas import tpu as pltpu
from jax.sharding import PartitionSpec as P

MESH = pl.DeviceIdType.MESH
ACQ = 16
SLOTS = 4
LINES = 20
TILES = 20
WIDE = TILES + 1
COMBOS = ((1, 0), (1, 1), (1, 2), (2, 0), (2, 1), (3, 0))
FORWARD = 5
TURN = 16
EDGE = 3
CROSS = 2 * 3 * SLOTS
EARLY = CROSS + ACQ
LATE = 2 * len(COMBOS)
PITCH = 24
ROWS = LINES * WIDE * 2
F32 = jnp.float32
BF16 = jnp.bfloat16


def kernel(
    acq, ref_hbm, sec_hbm, totals,
    block, edge, wide, wide_edge, table,
    sums, lhs, early, late,
    out_a, out_b, in_a, in_b, late_a, late_b, in_late_a, in_late_b,
    ref_own, sec_own, ref_prev, sec_prev, ref_next, sec_next,
    local_sem, slab_send, slab_recv,
    tile_send, tile_recv, index_send, index_recv, back_send, back_recv, late_send, late_recv, ready,
):
    d = lax.axis_index("pair")
    az = lax.axis_index("az")
    rg = lax.axis_index("rg")
    n = lax.axis_size("pair")
    oaz = 1 - az
    org = 1 - rg

    def at(step):
        return lax.rem(d + step + n, n)

    prev, nxt = at(-1), at(1)
    base = ACQ * d
    upper = az == 0

    own = [
        pltpu.make_async_copy(acq, block.at[:, :, pl.ds(0, TILES)], local_sem.at[0]),
        pltpu.make_async_copy(ref_hbm, ref_own, local_sem.at[1]),
        pltpu.make_async_copy(sec_hbm, sec_own, local_sem.at[2]),
    ]
    for copy in own:
        copy.start()

    barrier = pltpu.get_barrier_semaphore()
    peers = [
        (d, az, org), (d, oaz, rg),
        (prev, az, rg), (prev, az, org), (prev, oaz, rg),
    ]
    for peer in peers:
        pl.semaphore_signal(barrier, inc=1, device_id=peer, device_id_type=MESH)

    pl.semaphore_wait(barrier, len(peers))
    for peer in ((nxt, az, rg), (nxt, oaz, rg), (nxt, az, org)):
        pl.semaphore_signal(ready, inc=1, device_id=peer, device_id_type=MESH)

    def remote(src, dst, send, recv, device):
        return pltpu.make_async_remote_copy(
            src_ref=src, dst_ref=dst, send_sem=send, recv_sem=recv,
            device_id=device, device_id_type=MESH,
        )

    slabs = [
        remote(acq.at[ACQ - 2], edge.at[0, :, pl.ds(0, TILES)],
               slab_send.at[0], slab_recv.at[0], (nxt, az, rg)),
        remote(acq.at[ACQ - 1], edge.at[1, :, pl.ds(0, TILES)],
               slab_send.at[1], slab_recv.at[1], (nxt, az, rg)),
        remote(acq.at[0], edge.at[2, :, pl.ds(0, TILES)],
               slab_send.at[2], slab_recv.at[2], (prev, az, rg)),
    ]
    border = (TILES - 1) * org
    tiles = [
        remote(acq.at[:, :, border], block.at[:, :, TILES],
               tile_send.at[0], tile_recv.at[0], (d, az, org)),
        remote(acq.at[pl.ds(ACQ - 2, 2), :, border], edge.at[pl.ds(0, 2), :, TILES],
               tile_send.at[1], tile_recv.at[1], (nxt, az, org)),
        remote(acq.at[0, :, border], edge.at[2, :, TILES],
               tile_send.at[2], tile_recv.at[2], (prev, az, org)),
    ]
    indices = [
        remote(ref_hbm, ref_next, index_send.at[0], index_recv.at[0], (prev, az, rg)),
        remote(sec_hbm, sec_next, index_send.at[1], index_recv.at[1], (prev, az, rg)),
        remote(ref_hbm, ref_prev, index_send.at[2], index_recv.at[2], (nxt, az, rg)),
        remote(sec_hbm, sec_prev, index_send.at[3], index_recv.at[3], (nxt, az, rg)),
    ]
    for copy in indices[2:]:
        copy.start()
    for copy in tiles[:2]:
        copy.start()
    for a in (1, 0):
        slabs[a].start()

    col = lax.broadcasted_iota(jnp.int32, (128, 128), 1) * 20
    row = lax.broadcasted_iota(jnp.int32, (128, 128), 0)
    for t in range(WIDE):
        sample = row + 128 * t
        if t == TILES:
            sample = sample - (128 * WIDE) * rg
        inside = (sample >= col - 10) & (sample <= col + 30)
        table[pl.ds(128 * t, 128), :] = jnp.where(inside, 1.0, 0.0).astype(BF16)

    def line(ref, a, l):
        start = a * ROWS + l * (2 * WIDE)
        return (
            ref[pl.ds(start, WIDE, stride=2), :],
            ref[pl.ds(start + 1, WIDE, stride=2), :],
        )

    def put(plane, window, value):
        start = pl.multiple_of((plane * 8 + window) * PITCH, 8)
        sums[pl.ds(start, WIDE), :] = value

    def line_sums(plane, get):
        def add(*terms):
            total = terms[0]
            for term in terms[1:]:
                total = tuple(x + y for x, y in zip(total, term))
            return total

        def store(window, value):
            for i, v in enumerate(value):
                put(plane + i, window, v)

        l2 = None
        s0 = add(get(0), get(1))
        l2 = get(2)
        up = add(s0, l2)
        s3 = add(get(3), get(4), get(5), get(6))
        l7 = get(7)
        m1 = add(s3, l7)
        store(0, add(up, m1))
        s8 = add(get(8), get(9), get(10), get(11))
        l12 = get(12)
        m2 = add(s8, l12)
        store(1, add(l2, m1, m2))
        s13 = add(get(13), get(14), get(15), get(16))
        l17 = get(17)
        m3 = add(s13, l17)
        store(2, add(l7, m2, m3))
        down = add(l17, get(18), get(19))
        store(3, add(l12, s13, down))
        store(4, tuple(jnp.where(upper, x, y) for x, y in zip(down, up)))

    def power(plane, a):
        def get(l):
            x, y = line(wide, a, l)
            return (x * x + y * y,)
        line_sums(plane, get)

    def cross(plane, one, a, two, b):
        def get(l):
            xr, yr = line(one, a, l)
            xs, ys = line(two, b, l)
            return (xr * xs + yr * ys, yr * xs - xr * ys)
        line_sums(plane, get)

    def range_sums(first, planes, result):
        rows = planes * 8
        for t in range(WIDE):
            v = sums[pl.ds(first * 8 * PITCH + t, rows, stride=PITCH), :]
            hi = v.astype(BF16)
            lo = (v - hi.astype(F32)).astype(BF16)
            lhs[pl.ds(0, rows), pl.ds(128 * t, 128)] = hi
            lhs[pl.ds(rows, rows), pl.ds(128 * t, 128)] = lo
        both = jnp.dot(lhs[pl.ds(0, 2 * rows), :], table[...], preferred_element_type=F32)
        total = both[:rows] + both[rows:]
        result[pl.ds(first, planes)] = total.reshape(planes, 8, 128)

    own[0].wait()
    tiles[0].wait_recv()

    def widen(a, carry):
        start = pl.multiple_of(a * ROWS, 8)
        wide[pl.ds(start, ROWS), :] = block[a].reshape(ROWS, 128).astype(F32)
        return carry

    lax.fori_loop(0, ACQ, widen, 0)

    def power_step(a, carry):
        power(CROSS + a, a)
        return carry

    lax.fori_loop(0, ACQ, power_step, 0)

    for copy in own[1:]:
        copy.wait()
    names = [(ref_prev, sec_prev), (ref_own, sec_own), (ref_next, sec_next)]

    def clip(i):
        return jnp.clip(i, 0, ACQ - 1)

    def group(g):
        refs, secs = names[g]

        def cross_step(k, carry):
            cross(2 * (SLOTS * g + k), wide, clip(refs[k] - base), wide, clip(secs[k] - base))
            return carry

        lax.fori_loop(0, SLOTS, cross_step, 0)

    group(1)
    pl.semaphore_wait(ready, 3)
    for copy in indices[:2]:
        copy.start()
    tiles[2].start()
    slabs[2].start()
    for copy in indices[2:]:
        copy.wait_recv()
    group(0)
    for copy in indices[:2]:
        copy.wait_recv()
    group(2)

    range_sums(0, EARLY, early)

    zero = jnp.zeros((8, 128), F32)

    def collect(g, behind):
        refs, secs = names[g]
        for k in range(SLOTS):
            r = refs[k] - base
            s = secs[k] - base
            has_r = (r >= 0) & (r < ACQ)
            has_s = (s >= 0) & (s < ACQ)
            reach = ((r == -1) | (r == -2)) & has_s
            combo = jnp.clip(jnp.where(r == -1, s, s + 3), 0, FORWARD - 1)
            for c in range(4):
                if c < 2:
                    value = jnp.where(has_r & has_s, early[2 * (SLOTS * g + k) + c], zero)
                    if behind:
                        value = value + jnp.where(reach, late[2 * combo + c], zero)
                elif c == 2:
                    value = jnp.where(has_r, early[CROSS + clip(r)], zero)
                else:
                    value = jnp.where(has_s, early[CROSS + clip(s)], zero)
                out_a[g, 4 * k + c] = value[0:4]
                out_b[g, pl.ds(4 * k + c, 1), :] = value[4:5]

    collect(2, False)
    backs = [
        remote(out_a.at[2], in_a.at[0], back_send.at[0], back_recv.at[0], (nxt, az, rg)),
        remote(out_b.at[2], in_b.at[0], back_send.at[1], back_recv.at[1], (nxt, oaz, rg)),
        remote(out_a.at[0], in_a.at[1], back_send.at[2], back_recv.at[2], (prev, az, rg)),
        remote(out_b.at[0], in_b.at[2], back_send.at[3], back_recv.at[3], (prev, oaz, rg)),
        remote(out_b.at[1], in_b.at[1], back_send.at[4], back_recv.at[4], (d, oaz, rg)),
    ]
    for copy in backs[:2]:
        copy.start()

    def widen_edge(a):
        slabs[a].wait_recv()
        wide_edge[pl.ds(a * ROWS, ROWS), :] = edge[a].reshape(ROWS, 128).astype(F32)

    lates = [
        remote(late_a.at[1], in_late_a, late_send.at[0], late_recv.at[0], (nxt, az, rg)),
        remote(late_b.at[1], in_late_b, late_send.at[1], late_recv.at[1], (nxt, oaz, rg)),
    ]

    def reach_back():
        tiles[1].wait_recv()
        for a, far in ((1, 1), (0, 2)):
            widen_edge(a)
            for i, (r, s) in enumerate(COMBOS[:FORWARD]):
                if r == far:
                    cross(2 * i, wide_edge, a, wide, s)
        range_sums(0, 2 * FORWARD, late)
        collect(0, True)
        for copy in backs[2:4]:
            copy.start()
        collect(1, True)

    def reach_ahead():
        tiles[2].wait_recv()
        widen_edge(2)
        cross(2 * FORWARD, wide, ACQ - 3, wide_edge, 2)
        range_sums(2 * FORWARD, 2, late)
        for g in (2, 1):
            refs, secs = names[g]
            for k in range(SLOTS):
                reach = (refs[k] - base == ACQ - 3) & (secs[k] - base == ACQ)
                for c in range(2):
                    value = jnp.where(reach, late[2 * FORWARD + c], zero)
                    late_a[g - 1, 2 * k + c] = value[0:4]
                    late_b[g - 1, pl.ds(2 * k + c, 1), :] = value[4:5]
            if g == 2:
                for copy in lates:
                    copy.start()

    turned = lax.rem(d, TURN) == TURN - 1
    pl.when(turned)(reach_ahead)
    reach_back()
    pl.when(jnp.logical_not(turned))(reach_ahead)

    for k in range(SLOTS):
        for c in range(2):
            i, j = 4 * k + c, 2 * k + c
            out_a[1, i] = out_a[1, i] + late_a[0, j]
            out_b[1, pl.ds(i, 1), :] = out_b[1, pl.ds(i, 1), :] + late_b[0, pl.ds(j, 1), :]
    backs[4].start()
    for copy in tiles + indices + slabs:
        copy.wait_send()
    for copy in backs + lates:
        copy.wait()

    window = lax.broadcasted_iota(jnp.int32, (4, 128), 0)
    shared = window == 3 * oaz
    for k in range(SLOTS):
        for c in range(4):
            i = 4 * k + c
            rim = in_b[0, pl.ds(i, 1), :] + in_b[1, pl.ds(i, 1), :] + in_b[2, pl.ds(i, 1), :]
            body = out_a[1, i] + in_a[0, i] + in_a[1, i]
            if c < 2:
                j = 2 * k + c
                rim = rim + in_late_b[pl.ds(j, 1), :]
                body = body + in_late_a[j]
            totals[k, c] = body + jnp.where(shared, rim, 0.0)


def finish(totals, count, ifg, coh):
    slot = lax.broadcasted_iota(jnp.int32, (SLOTS, 4, 128), 0)
    live = slot < count[...].reshape(1, 1, 1)
    re, im = totals[:, 0], totals[:, 1]
    value = jnp.sqrt(re * re + im * im) / jnp.sqrt(totals[:, 2] * totals[:, 3] + 1e-06)
    ifg[:, 0] = jnp.where(live, re / 451.0, 0.0)
    ifg[:, 1] = jnp.where(live, im / 451.0, 0.0)
    coh[...] = jnp.where(live, value, 0.0)


def on_device(acquisitions, reference_index, secondary_index, pair_count):
    view = acquisitions.reshape(ACQ, 2, LINES, TILES, 128)
    view = with_layout_constraint(view, Layout((0, 2, 3, 1, 4)))
    view = view.transpose(0, 2, 3, 1, 4)
    hbm = pl.BlockSpec(memory_space=pltpu.HBM)
    vmem = pl.BlockSpec(memory_space=pltpu.VMEM)
    dma = pltpu.SemaphoreType.DMA
    totals = pl.pallas_call(
        kernel,
        out_shape=pltpu.VMEM((SLOTS, 4, 4, 128), F32),
        in_specs=[hbm] * 3,
        out_specs=vmem,
        scratch_shapes=[
            pltpu.VMEM((ACQ, LINES, WIDE, 2, 128), BF16),
            pltpu.VMEM((EDGE, LINES, WIDE, 2, 128), BF16),
            pltpu.VMEM((ACQ * ROWS, 128), F32),
            pltpu.VMEM((EDGE * ROWS, 128), F32),
            pltpu.VMEM((128 * WIDE, 128), BF16),
            pltpu.VMEM((EARLY * 8 * PITCH, 128), F32),
            pltpu.VMEM((EARLY * 16, 128 * WIDE), BF16),
            pltpu.VMEM((EARLY, 8, 128), F32),
            pltpu.VMEM((LATE, 8, 128), F32),
            pltpu.VMEM((3, 16, 4, 128), F32),
            pltpu.VMEM((3, 16, 128), F32),
            pltpu.VMEM((2, 16, 4, 128), F32),
            pltpu.VMEM((3, 16, 128), F32),
            pltpu.VMEM((2, 8, 4, 128), F32),
            pltpu.VMEM((2, 8, 128), F32),
            pltpu.VMEM((8, 4, 128), F32),
            pltpu.VMEM((8, 128), F32),
        ] + [pltpu.SMEM((SLOTS,), jnp.int32)] * 6 + [
            dma((3,)), dma((EDGE,)), dma((EDGE,)), dma((3,)), dma((3,)),
            dma((4,)), dma((4,)), dma((5,)), dma((5,)), dma((2,)), dma((2,)),
            pltpu.SemaphoreType.REGULAR,
        ],
        compiler_params=pltpu.CompilerParams(
            collective_id=0, has_side_effects=True, vmem_limit_bytes=60 * 2**20
        ),
    )(view, reference_index, secondary_index)
    return pl.pallas_call(
        finish,
        out_shape=(
            jax.ShapeDtypeStruct((SLOTS, 2, 4, 128), F32),
            jax.ShapeDtypeStruct((SLOTS, 4, 128), F32),
        ),
        in_specs=[vmem, vmem],
        out_specs=(vmem, vmem),
        compiler_params=pltpu.CompilerParams(vmem_limit_bytes=2**20),
    )(totals, pair_count.reshape(1, 1))


def solution(mesh):
    return jax.shard_map(
        on_device,
        mesh=mesh,
        in_specs=(P("pair", None, "az", "rg"), P("pair"), P("pair"), P("pair")),
        out_specs=(P("pair", None, "az", "rg"), P("pair", "az", "rg")),
        check_vma=False,
    )
```

```python
import jax
import jax.numpy as jnp
from jax import lax
from jax.experimental import pallas as pl
from jax.experimental.layout import Layout, with_layout_constraint
from jax.experimental.pallas import tpu as pltpu
from jax.sharding import PartitionSpec as P

MESH = pl.DeviceIdType.MESH
ACQ = 16
SLOTS = 4
LINES = 20
TILES = 20
WIDE = TILES + 1
COMBOS = ((1, 0), (1, 1), (1, 2), (2, 0), (2, 1), (3, 0))
FORWARD = 5
TURN = 16
EDGE = 3
CROSS = 2 * 3 * SLOTS
EARLY = CROSS + ACQ
LATE = 2 * len(COMBOS)
PITCH = 24
ROWS = LINES * WIDE * 2
F32 = jnp.float32
BF16 = jnp.bfloat16


def kernel(
    acq, ref_hbm, sec_hbm, totals,
    block, edge, wide, wide_edge, table,
    sums, lhs, early, late,
    out_a, out_b, in_a, in_b, late_a, late_b, in_late_a, in_late_b,
    ref_own, sec_own, ref_prev, sec_prev, ref_next, sec_next,
    local_sem, slab_send, slab_recv,
    tile_send, tile_recv, index_send, index_recv, back_send, back_recv, late_send, late_recv, ready,
):
    d = lax.axis_index("pair")
    az = lax.axis_index("az")
    rg = lax.axis_index("rg")
    n = lax.axis_size("pair")
    oaz = 1 - az
    org = 1 - rg

    def at(step):
        return lax.rem(d + step + n, n)

    prev, nxt = at(-1), at(1)
    base = ACQ * d
    upper = az == 0

    own = [
        pltpu.make_async_copy(acq, block.at[:, :, pl.ds(0, TILES)], local_sem.at[0]),
        pltpu.make_async_copy(ref_hbm, ref_own, local_sem.at[1]),
        pltpu.make_async_copy(sec_hbm, sec_own, local_sem.at[2]),
    ]
    for copy in own:
        copy.start()

    barrier = pltpu.get_barrier_semaphore()
    peers = [
        (d, az, org), (d, oaz, rg),
        (prev, az, rg), (prev, az, org), (prev, oaz, rg),
    ]
    for peer in peers:
        pl.semaphore_signal(barrier, inc=1, device_id=peer, device_id_type=MESH)

    pl.semaphore_wait(barrier, len(peers))
    for peer in ((nxt, az, rg), (nxt, oaz, rg), (nxt, az, org)):
        pl.semaphore_signal(ready, inc=1, device_id=peer, device_id_type=MESH)

    def remote(src, dst, send, recv, device):
        return pltpu.make_async_remote_copy(
            src_ref=src, dst_ref=dst, send_sem=send, recv_sem=recv,
            device_id=device, device_id_type=MESH,
        )

    slabs = [
        remote(acq.at[ACQ - 2], edge.at[0, :, pl.ds(0, TILES)],
               slab_send.at[0], slab_recv.at[0], (nxt, az, rg)),
        remote(acq.at[ACQ - 1], edge.at[1, :, pl.ds(0, TILES)],
               slab_send.at[1], slab_recv.at[1], (nxt, az, rg)),
        remote(acq.at[0], edge.at[2, :, pl.ds(0, TILES)],
               slab_send.at[2], slab_recv.at[2], (prev, az, rg)),
    ]
    border = (TILES - 1) * org
    tiles = [
        remote(acq.at[:, :, border], block.at[:, :, TILES],
               tile_send.at[0], tile_recv.at[0], (d, az, org)),
        remote(acq.at[pl.ds(ACQ - 2, 2), :, border], edge.at[pl.ds(0, 2), :, TILES],
               tile_send.at[1], tile_recv.at[1], (nxt, az, org)),
        remote(acq.at[0, :, border], edge.at[2, :, TILES],
               tile_send.at[2], tile_recv.at[2], (prev, az, org)),
    ]
    indices = [
        remote(ref_hbm, ref_next, index_send.at[0], index_recv.at[0], (prev, az, rg)),
        remote(sec_hbm, sec_next, index_send.at[1], index_recv.at[1], (prev, az, rg)),
        remote(ref_hbm, ref_prev, index_send.at[2], index_recv.at[2], (nxt, az, rg)),
        remote(sec_hbm, sec_prev, index_send.at[3], index_recv.at[3], (nxt, az, rg)),
    ]
    for copy in indices[2:]:
        copy.start()
    for copy in tiles[:2]:
        copy.start()
    for a in (1, 0):
        slabs[a].start()

    col = lax.broadcasted_iota(jnp.int32, (128, 128), 1) * 20
    row = lax.broadcasted_iota(jnp.int32, (128, 128), 0)
    for t in range(WIDE):
        sample = row + 128 * t
        if t == TILES:
            sample = sample - (128 * WIDE) * rg
        inside = (sample >= col - 10) & (sample <= col + 30)
        table[pl.ds(128 * t, 128), :] = jnp.where(inside, 1.0, 0.0).astype(BF16)

    def line(ref, a, l):
        start = a * ROWS + l * (2 * WIDE)
        return (
            ref[pl.ds(start, WIDE, stride=2), :],
            ref[pl.ds(start + 1, WIDE, stride=2), :],
        )

    def put(plane, window, value):
        start = pl.multiple_of((plane * 8 + window) * PITCH, 8)
        sums[pl.ds(start, WIDE), :] = value

    def line_sums(plane, get):
        def add(*terms):
            total = terms[0]
            for term in terms[1:]:
                total = tuple(x + y for x, y in zip(total, term))
            return total

        def store(window, value):
            for i, v in enumerate(value):
                put(plane + i, window, v)

        l2 = None
        s0 = add(get(0), get(1))
        l2 = get(2)
        up = add(s0, l2)
        s3 = add(get(3), get(4), get(5), get(6))
        l7 = get(7)
        m1 = add(s3, l7)
        store(0, add(up, m1))
        s8 = add(get(8), get(9), get(10), get(11))
        l12 = get(12)
        m2 = add(s8, l12)
        store(1, add(l2, m1, m2))
        s13 = add(get(13), get(14), get(15), get(16))
        l17 = get(17)
        m3 = add(s13, l17)
        store(2, add(l7, m2, m3))
        down = add(l17, get(18), get(19))
        store(3, add(l12, s13, down))
        store(4, tuple(jnp.where(upper, x, y) for x, y in zip(down, up)))

    def power(plane, a):
        def get(l):
            x, y = line(wide, a, l)
            return (x * x + y * y,)
        line_sums(plane, get)

    def cross(plane, one, a, two, b):
        def get(l):
            xr, yr = line(one, a, l)
            xs, ys = line(two, b, l)
            return (xr * xs + yr * ys, yr * xs - xr * ys)
        line_sums(plane, get)

    def range_sums(first, planes, result):
        rows = planes * 8
        for t in range(WIDE):
            v = sums[pl.ds(first * 8 * PITCH + t, rows, stride=PITCH), :]
            hi = v.astype(BF16)
            lo = (v - hi.astype(F32)).astype(BF16)
            lhs[pl.ds(0, rows), pl.ds(128 * t, 128)] = hi
            lhs[pl.ds(rows, rows), pl.ds(128 * t, 128)] = lo
        both = jnp.dot(lhs[pl.ds(0, 2 * rows), :], table[...], preferred_element_type=F32)
        total = both[:rows] + both[rows:]
        result[pl.ds(first, planes)] = total.reshape(planes, 8, 128)

    def send_back():
        pl.semaphore_wait(ready, 3)
        for copy in indices[:2]:
            copy.start()
        tiles[2].start()
        slabs[2].start()

    soon = lax.rem(d, 2) == 1
    pl.when(soon)(send_back)

    own[0].wait()
    tiles[0].wait_recv()

    def widen(a, carry):
        start = pl.multiple_of(a * ROWS, 8)
        wide[pl.ds(start, ROWS), :] = block[a].reshape(ROWS, 128).astype(F32)
        return carry

    lax.fori_loop(0, ACQ, widen, 0)

    def power_step(a, carry):
        power(CROSS + a, a)
        return carry

    lax.fori_loop(0, ACQ, power_step, 0)

    for copy in own[1:]:
        copy.wait()
    names = [(ref_prev, sec_prev), (ref_own, sec_own), (ref_next, sec_next)]

    def clip(i):
        return jnp.clip(i, 0, ACQ - 1)

    def group(g):
        refs, secs = names[g]

        def cross_step(k, carry):
            cross(2 * (SLOTS * g + k), wide, clip(refs[k] - base), wide, clip(secs[k] - base))
            return carry

        lax.fori_loop(0, SLOTS, cross_step, 0)

    group(1)
    pl.when(jnp.logical_not(soon))(send_back)
    for copy in indices[2:]:
        copy.wait_recv()
    group(0)
    for copy in indices[:2]:
        copy.wait_recv()
    group(2)

    range_sums(0, EARLY, early)

    zero = jnp.zeros((8, 128), F32)

    def collect(g, behind):
        refs, secs = names[g]
        for k in range(SLOTS):
            r = refs[k] - base
            s = secs[k] - base
            has_r = (r >= 0) & (r < ACQ)
            has_s = (s >= 0) & (s < ACQ)
            reach = ((r == -1) | (r == -2)) & has_s
            combo = jnp.clip(jnp.where(r == -1, s, s + 3), 0, FORWARD - 1)
            for c in range(4):
                if c < 2:
                    value = jnp.where(has_r & has_s, early[2 * (SLOTS * g + k) + c], zero)
                    if behind:
                        value = value + jnp.where(reach, late[2 * combo + c], zero)
                elif c == 2:
                    value = jnp.where(has_r, early[CROSS + clip(r)], zero)
                else:
                    value = jnp.where(has_s, early[CROSS + clip(s)], zero)
                out_a[g, 4 * k + c] = value[0:4]
                out_b[g, pl.ds(4 * k + c, 1), :] = value[4:5]

    collect(2, False)
    backs = [
        remote(out_a.at[2], in_a.at[0], back_send.at[0], back_recv.at[0], (nxt, az, rg)),
        remote(out_b.at[2], in_b.at[0], back_send.at[1], back_recv.at[1], (nxt, oaz, rg)),
        remote(out_a.at[0], in_a.at[1], back_send.at[2], back_recv.at[2], (prev, az, rg)),
        remote(out_b.at[0], in_b.at[2], back_send.at[3], back_recv.at[3], (prev, oaz, rg)),
        remote(out_b.at[1], in_b.at[1], back_send.at[4], back_recv.at[4], (d, oaz, rg)),
    ]
    for copy in backs[:2]:
        copy.start()

    def widen_edge(a):
        slabs[a].wait_recv()
        wide_edge[pl.ds(a * ROWS, ROWS), :] = edge[a].reshape(ROWS, 128).astype(F32)

    lates = [
        remote(late_a.at[1], in_late_a, late_send.at[0], late_recv.at[0], (nxt, az, rg)),
        remote(late_b.at[1], in_late_b, late_send.at[1], late_recv.at[1], (nxt, oaz, rg)),
    ]

    def reach_back():
        tiles[1].wait_recv()
        for a, far in ((1, 1), (0, 2)):
            widen_edge(a)
            for i, (r, s) in enumerate(COMBOS[:FORWARD]):
                if r == far:
                    cross(2 * i, wide_edge, a, wide, s)
        range_sums(0, 2 * FORWARD, late)
        collect(0, True)
        for copy in backs[2:4]:
            copy.start()
        collect(1, True)

    def reach_ahead():
        tiles[2].wait_recv()
        widen_edge(2)
        cross(2 * FORWARD, wide, ACQ - 3, wide_edge, 2)
        range_sums(2 * FORWARD, 2, late)
        for g in (2, 1):
            refs, secs = names[g]
            for k in range(SLOTS):
                reach = (refs[k] - base == ACQ - 3) & (secs[k] - base == ACQ)
                for c in range(2):
                    value = jnp.where(reach, late[2 * FORWARD + c], zero)
                    late_a[g - 1, 2 * k + c] = value[0:4]
                    late_b[g - 1, pl.ds(2 * k + c, 1), :] = value[4:5]
            if g == 2:
                for copy in lates:
                    copy.start()

    turned = lax.rem(d, TURN) == TURN - 1
    pl.when(turned)(reach_ahead)
    reach_back()
    pl.when(jnp.logical_not(turned))(reach_ahead)

    for k in range(SLOTS):
        for c in range(2):
            i, j = 4 * k + c, 2 * k + c
            out_a[1, i] = out_a[1, i] + late_a[0, j]
            out_b[1, pl.ds(i, 1), :] = out_b[1, pl.ds(i, 1), :] + late_b[0, pl.ds(j, 1), :]
    backs[4].start()
    for copy in tiles + indices + slabs:
        copy.wait_send()
    for copy in backs + lates:
        copy.wait()

    window = lax.broadcasted_iota(jnp.int32, (4, 128), 0)
    shared = window == 3 * oaz
    for k in range(SLOTS):
        for c in range(4):
            i = 4 * k + c
            rim = in_b[0, pl.ds(i, 1), :] + in_b[1, pl.ds(i, 1), :] + in_b[2, pl.ds(i, 1), :]
            body = out_a[1, i] + in_a[0, i] + in_a[1, i]
            if c < 2:
                j = 2 * k + c
                rim = rim + in_late_b[pl.ds(j, 1), :]
                body = body + in_late_a[j]
            totals[k, c] = body + jnp.where(shared, rim, 0.0)


def finish(totals, count, ifg, coh):
    slot = lax.broadcasted_iota(jnp.int32, (SLOTS, 4, 128), 0)
    live = slot < count[...].reshape(1, 1, 1)
    re, im = totals[:, 0], totals[:, 1]
    value = jnp.sqrt(re * re + im * im) / jnp.sqrt(totals[:, 2] * totals[:, 3] + 1e-06)
    ifg[:, 0] = jnp.where(live, re / 451.0, 0.0)
    ifg[:, 1] = jnp.where(live, im / 451.0, 0.0)
    coh[...] = jnp.where(live, value, 0.0)


def on_device(acquisitions, reference_index, secondary_index, pair_count):
    view = acquisitions.reshape(ACQ, 2, LINES, TILES, 128)
    view = with_layout_constraint(view, Layout((0, 2, 3, 1, 4)))
    view = view.transpose(0, 2, 3, 1, 4)
    hbm = pl.BlockSpec(memory_space=pltpu.HBM)
    vmem = pl.BlockSpec(memory_space=pltpu.VMEM)
    dma = pltpu.SemaphoreType.DMA
    totals = pl.pallas_call(
        kernel,
        out_shape=pltpu.VMEM((SLOTS, 4, 4, 128), F32),
        in_specs=[hbm] * 3,
        out_specs=vmem,
        scratch_shapes=[
            pltpu.VMEM((ACQ, LINES, WIDE, 2, 128), BF16),
            pltpu.VMEM((EDGE, LINES, WIDE, 2, 128), BF16),
            pltpu.VMEM((ACQ * ROWS, 128), F32),
            pltpu.VMEM((EDGE * ROWS, 128), F32),
            pltpu.VMEM((128 * WIDE, 128), BF16),
            pltpu.VMEM((EARLY * 8 * PITCH, 128), F32),
            pltpu.VMEM((EARLY * 16, 128 * WIDE), BF16),
            pltpu.VMEM((EARLY, 8, 128), F32),
            pltpu.VMEM((LATE, 8, 128), F32),
            pltpu.VMEM((3, 16, 4, 128), F32),
            pltpu.VMEM((3, 16, 128), F32),
            pltpu.VMEM((2, 16, 4, 128), F32),
            pltpu.VMEM((3, 16, 128), F32),
            pltpu.VMEM((2, 8, 4, 128), F32),
            pltpu.VMEM((2, 8, 128), F32),
            pltpu.VMEM((8, 4, 128), F32),
            pltpu.VMEM((8, 128), F32),
        ] + [pltpu.SMEM((SLOTS,), jnp.int32)] * 6 + [
            dma((3,)), dma((EDGE,)), dma((EDGE,)), dma((3,)), dma((3,)),
            dma((4,)), dma((4,)), dma((5,)), dma((5,)), dma((2,)), dma((2,)),
            pltpu.SemaphoreType.REGULAR,
        ],
        compiler_params=pltpu.CompilerParams(
            collective_id=0, has_side_effects=True, vmem_limit_bytes=60 * 2**20
        ),
    )(view, reference_index, secondary_index)
    return pl.pallas_call(
        finish,
        out_shape=(
            jax.ShapeDtypeStruct((SLOTS, 2, 4, 128), F32),
            jax.ShapeDtypeStruct((SLOTS, 4, 128), F32),
        ),
        in_specs=[vmem, vmem],
        out_specs=(vmem, vmem),
        compiler_params=pltpu.CompilerParams(vmem_limit_bytes=2**20),
    )(totals, pair_count.reshape(1, 1))


def solution(mesh):
    return jax.shard_map(
        on_device,
        mesh=mesh,
        in_specs=(P("pair", None, "az", "rg"), P("pair"), P("pair"), P("pair")),
        out_specs=(P("pair", None, "az", "rg"), P("pair", "az", "rg")),
        check_vma=False,
    )
```

```python
import functools

import jax
import jax.numpy as jnp
from jax import lax
from jax.experimental import pallas as pl
from jax.experimental.layout import Layout, with_layout_constraint
from jax.experimental.pallas import tpu as pltpu
from jax.sharding import PartitionSpec as P

MESH = pl.DeviceIdType.MESH
ACQ = 16
SLOTS = 4
LINES = 20
TILES = 20
WIDE = TILES + 1
COMBOS = ((1, 0), (1, 1), (1, 2), (2, 0), (2, 1), (3, 0))
FORWARD = 5
TURN = 16
EDGE = 3
CROSS = 2 * 3 * SLOTS
EARLY = CROSS + ACQ
LATE = 2 * len(COMBOS)
PITCH = 24
ROWS = LINES * WIDE * 2
F32 = jnp.float32
BF16 = jnp.bfloat16


def kernel(
    acq, ref_hbm, sec_hbm, totals,
    block, edge, wide, wide_edge, table,
    sums, lhs, early, late,
    out_a, out_b, in_a, in_b, late_a, late_b, in_late_a, in_late_b,
    ref_own, sec_own, ref_prev, sec_prev, ref_next, sec_next,
    local_sem, slab_send, slab_recv,
    tile_send, tile_recv, index_send, index_recv, back_send, back_recv, late_send, late_recv, ready,
):
    d = lax.axis_index("pair")
    az = lax.axis_index("az")
    rg = lax.axis_index("rg")
    n = lax.axis_size("pair")
    oaz = 1 - az
    org = 1 - rg

    def at(step):
        return lax.rem(d + step + n, n)

    prev, nxt = at(-1), at(1)
    base = ACQ * d
    has_prev, has_next = d > 0, d < n - 1
    upper = az == 0

    own = [
        pltpu.make_async_copy(acq, block.at[:, :, pl.ds(0, TILES)], local_sem.at[0]),
        pltpu.make_async_copy(ref_hbm, ref_own, local_sem.at[1]),
        pltpu.make_async_copy(sec_hbm, sec_own, local_sem.at[2]),
    ]
    for copy in own:
        copy.start()

    barrier = pltpu.get_barrier_semaphore()
    def greet(semaphore, peers):
        for peer in peers:
            pl.semaphore_signal(semaphore, inc=1, device_id=peer, device_id_type=MESH)

    greet(barrier, [(d, az, org), (d, oaz, rg)])

    @pl.when(has_prev)
    def _():
        greet(barrier, [(prev, az, rg), (prev, az, org), (prev, oaz, rg)])

    pl.semaphore_wait(barrier, jnp.where(has_next, 5, 2))

    @pl.when(has_next)
    def _():
        greet(ready, [(nxt, az, rg), (nxt, oaz, rg), (nxt, az, org)])

    def remote(src, dst, send, recv, device):
        return pltpu.make_async_remote_copy(
            src_ref=src, dst_ref=dst, send_sem=send, recv_sem=recv,
            device_id=device, device_id_type=MESH,
        )

    class Toward:
        def __init__(self, step, *parts):
            self.copy = remote(*parts)
            self.sends, self.receives = (
                (has_next, has_prev) if step > 0 else (has_prev, has_next)
            )

        def start(self):
            pl.when(self.sends)(self.copy.start)

        def wait_send(self):
            pl.when(self.sends)(self.copy.wait_send)

        def wait_recv(self):
            pl.when(self.receives)(self.copy.wait_recv)

        def wait(self):
            self.wait_send()
            self.wait_recv()

    forward = functools.partial(Toward, 1)
    backward = functools.partial(Toward, -1)

    @pl.when(jnp.logical_not(has_prev))
    def _():
        for ref in (in_a.at[0], in_b.at[0], in_late_a, in_late_b):
            ref[...] = jnp.zeros(ref.shape, F32)
        for k in range(SLOTS):
            ref_prev[k] = 0
            sec_prev[k] = 0

    @pl.when(jnp.logical_not(has_next))
    def _():
        for ref in (in_a.at[1], in_b.at[2]):
            ref[...] = jnp.zeros(ref.shape, F32)
        for k in range(SLOTS):
            ref_next[k] = 0
            sec_next[k] = 0

    slabs = [
        forward(acq.at[ACQ - 2], edge.at[0, :, pl.ds(0, TILES)],
               slab_send.at[0], slab_recv.at[0], (nxt, az, rg)),
        forward(acq.at[ACQ - 1], edge.at[1, :, pl.ds(0, TILES)],
               slab_send.at[1], slab_recv.at[1], (nxt, az, rg)),
        backward(acq.at[0], edge.at[2, :, pl.ds(0, TILES)],
               slab_send.at[2], slab_recv.at[2], (prev, az, rg)),
    ]
    border = (TILES - 1) * org
    tiles = [
        remote(acq.at[:, :, border], block.at[:, :, TILES],
               tile_send.at[0], tile_recv.at[0], (d, az, org)),
        forward(acq.at[pl.ds(ACQ - 2, 2), :, border], edge.at[pl.ds(0, 2), :, TILES],
               tile_send.at[1], tile_recv.at[1], (nxt, az, org)),
        backward(acq.at[0, :, border], edge.at[2, :, TILES],
               tile_send.at[2], tile_recv.at[2], (prev, az, org)),
    ]
    indices = [
        backward(ref_hbm, ref_next, index_send.at[0], index_recv.at[0], (prev, az, rg)),
        backward(sec_hbm, sec_next, index_send.at[1], index_recv.at[1], (prev, az, rg)),
        forward(ref_hbm, ref_prev, index_send.at[2], index_recv.at[2], (nxt, az, rg)),
        forward(sec_hbm, sec_prev, index_send.at[3], index_recv.at[3], (nxt, az, rg)),
    ]
    for copy in indices[2:]:
        copy.start()
    for copy in tiles[:2]:
        copy.start()
    for a in (1, 0):
        slabs[a].start()

    col = lax.broadcasted_iota(jnp.int32, (128, 128), 1) * 20
    row = lax.broadcasted_iota(jnp.int32, (128, 128), 0)
    for t in range(WIDE):
        sample = row + 128 * t
        if t == TILES:
            sample = sample - (128 * WIDE) * rg
        inside = (sample >= col - 10) & (sample <= col + 30)
        table[pl.ds(128 * t, 128), :] = jnp.where(inside, 1.0, 0.0).astype(BF16)

    def line(ref, a, l):
        start = a * ROWS + l * (2 * WIDE)
        return (
            ref[pl.ds(start, WIDE, stride=2), :],
            ref[pl.ds(start + 1, WIDE, stride=2), :],
        )

    def put(plane, window, value):
        start = pl.multiple_of((plane * 8 + window) * PITCH, 8)
        sums[pl.ds(start, WIDE), :] = value

    def line_sums(plane, get):
        def add(*terms):
            total = terms[0]
            for term in terms[1:]:
                total = tuple(x + y for x, y in zip(total, term))
            return total

        def store(window, value):
            for i, v in enumerate(value):
                put(plane + i, window, v)

        l2 = None
        s0 = add(get(0), get(1))
        l2 = get(2)
        up = add(s0, l2)
        s3 = add(get(3), get(4), get(5), get(6))
        l7 = get(7)
        m1 = add(s3, l7)
        store(0, add(up, m1))
        s8 = add(get(8), get(9), get(10), get(11))
        l12 = get(12)
        m2 = add(s8, l12)
        store(1, add(l2, m1, m2))
        s13 = add(get(13), get(14), get(15), get(16))
        l17 = get(17)
        m3 = add(s13, l17)
        store(2, add(l7, m2, m3))
        down = add(l17, get(18), get(19))
        store(3, add(l12, s13, down))
        store(4, tuple(jnp.where(upper, x, y) for x, y in zip(down, up)))

    def power(plane, a):
        def get(l):
            x, y = line(wide, a, l)
            return (x * x + y * y,)
        line_sums(plane, get)

    def cross(plane, one, a, two, b):
        def get(l):
            xr, yr = line(one, a, l)
            xs, ys = line(two, b, l)
            return (xr * xs + yr * ys, yr * xs - xr * ys)
        line_sums(plane, get)

    def range_sums(first, planes, result):
        rows = planes * 8
        for t in range(WIDE):
            v = sums[pl.ds(first * 8 * PITCH + t, rows, stride=PITCH), :]
            hi = v.astype(BF16)
            lo = (v - hi.astype(F32)).astype(BF16)
            lhs[pl.ds(0, rows), pl.ds(128 * t, 128)] = hi
            lhs[pl.ds(rows, rows), pl.ds(128 * t, 128)] = lo
        both = jnp.dot(lhs[pl.ds(0, 2 * rows), :], table[...], preferred_element_type=F32)
        total = both[:rows] + both[rows:]
        result[pl.ds(first, planes)] = total.reshape(planes, 8, 128)

    def send_back():
        pl.when(has_prev)(lambda: pl.semaphore_wait(ready, 3))
        for copy in indices[:2]:
            copy.start()
        tiles[2].start()
        slabs[2].start()

    soon = lax.rem(d, 2) == 1
    pl.when(soon)(send_back)

    own[0].wait()
    tiles[0].wait_recv()

    def widen(a, carry):
        start = pl.multiple_of(a * ROWS, 8)
        wide[pl.ds(start, ROWS), :] = block[a].reshape(ROWS, 128).astype(F32)
        return carry

    lax.fori_loop(0, ACQ, widen, 0)

    def power_step(a, carry):
        power(CROSS + a, a)
        return carry

    lax.fori_loop(0, ACQ, power_step, 0)

    for copy in own[1:]:
        copy.wait()
    names = [(ref_prev, sec_prev), (ref_own, sec_own), (ref_next, sec_next)]

    def clip(i):
        return jnp.clip(i, 0, ACQ - 1)

    def group(g):
        refs, secs = names[g]

        def cross_step(k, carry):
            cross(2 * (SLOTS * g + k), wide, clip(refs[k] - base), wide, clip(secs[k] - base))
            return carry

        lax.fori_loop(0, SLOTS, cross_step, 0)

    group(1)
    pl.when(jnp.logical_not(soon))(send_back)
    for copy in indices[2:]:
        copy.wait_recv()
    group(0)
    for copy in indices[:2]:
        copy.wait_recv()
    group(2)

    range_sums(0, EARLY, early)

    zero = jnp.zeros((8, 128), F32)

    def collect(g, behind):
        refs, secs = names[g]
        for k in range(SLOTS):
            r = refs[k] - base
            s = secs[k] - base
            has_r = (r >= 0) & (r < ACQ)
            has_s = (s >= 0) & (s < ACQ)
            reach = ((r == -1) | (r == -2)) & has_s
            combo = jnp.clip(jnp.where(r == -1, s, s + 3), 0, FORWARD - 1)
            for c in range(4):
                if c < 2:
                    value = jnp.where(has_r & has_s, early[2 * (SLOTS * g + k) + c], zero)
                    if behind:
                        value = value + jnp.where(reach, late[2 * combo + c], zero)
                elif c == 2:
                    value = jnp.where(has_r, early[CROSS + clip(r)], zero)
                else:
                    value = jnp.where(has_s, early[CROSS + clip(s)], zero)
                out_a[g, 4 * k + c] = value[0:4]
                out_b[g, pl.ds(4 * k + c, 1), :] = value[4:5]

    collect(2, False)
    backs = [
        forward(out_a.at[2], in_a.at[0], back_send.at[0], back_recv.at[0], (nxt, az, rg)),
        forward(out_b.at[2], in_b.at[0], back_send.at[1], back_recv.at[1], (nxt, oaz, rg)),
        backward(out_a.at[0], in_a.at[1], back_send.at[2], back_recv.at[2], (prev, az, rg)),
        backward(out_b.at[0], in_b.at[2], back_send.at[3], back_recv.at[3], (prev, oaz, rg)),
        remote(out_b.at[1], in_b.at[1], back_send.at[4], back_recv.at[4], (d, oaz, rg)),
    ]
    for copy in backs[:2]:
        copy.start()

    def widen_edge(a):
        slabs[a].wait_recv()
        wide_edge[pl.ds(a * ROWS, ROWS), :] = edge[a].reshape(ROWS, 128).astype(F32)

    lates = [
        forward(late_a.at[1], in_late_a, late_send.at[0], late_recv.at[0], (nxt, az, rg)),
        forward(late_b.at[1], in_late_b, late_send.at[1], late_recv.at[1], (nxt, oaz, rg)),
    ]

    def reach_back():
        tiles[1].wait_recv()
        for a, far in ((1, 1), (0, 2)):
            widen_edge(a)
            for i, (r, s) in enumerate(COMBOS[:FORWARD]):
                if r == far:
                    cross(2 * i, wide_edge, a, wide, s)
        range_sums(0, 2 * FORWARD, late)
        collect(0, True)
        for copy in backs[2:4]:
            copy.start()
        collect(1, True)

    def reach_ahead():
        tiles[2].wait_recv()
        widen_edge(2)
        cross(2 * FORWARD, wide, ACQ - 3, wide_edge, 2)
        range_sums(2 * FORWARD, 2, late)
        for g in (2, 1):
            refs, secs = names[g]
            for k in range(SLOTS):
                reach = (refs[k] - base == ACQ - 3) & (secs[k] - base == ACQ)
                for c in range(2):
                    value = jnp.where(reach, late[2 * FORWARD + c], zero)
                    late_a[g - 1, 2 * k + c] = value[0:4]
                    late_b[g - 1, pl.ds(2 * k + c, 1), :] = value[4:5]
            if g == 2:
                for copy in lates:
                    copy.start()

    turned = lax.rem(d, TURN) == TURN - 1
    pl.when(turned)(reach_ahead)
    reach_back()
    pl.when(jnp.logical_not(turned))(reach_ahead)

    for k in range(SLOTS):
        for c in range(2):
            i, j = 4 * k + c, 2 * k + c
            out_a[1, i] = out_a[1, i] + late_a[0, j]
            out_b[1, pl.ds(i, 1), :] = out_b[1, pl.ds(i, 1), :] + late_b[0, pl.ds(j, 1), :]
    backs[4].start()
    for copy in tiles + indices + slabs:
        copy.wait_send()
    for copy in backs + lates:
        copy.wait()

    window = lax.broadcasted_iota(jnp.int32, (4, 128), 0)
    shared = window == 3 * oaz
    for k in range(SLOTS):
        for c in range(4):
            i = 4 * k + c
            rim = in_b[0, pl.ds(i, 1), :] + in_b[1, pl.ds(i, 1), :] + in_b[2, pl.ds(i, 1), :]
            body = out_a[1, i] + in_a[0, i] + in_a[1, i]
            if c < 2:
                j = 2 * k + c
                rim = rim + in_late_b[pl.ds(j, 1), :]
                body = body + in_late_a[j]
            totals[k, c] = body + jnp.where(shared, rim, 0.0)


def finish(totals, count, ifg, coh):
    slot = lax.broadcasted_iota(jnp.int32, (SLOTS, 4, 128), 0)
    live = slot < count[...].reshape(1, 1, 1)
    re, im = totals[:, 0], totals[:, 1]
    value = jnp.sqrt(re * re + im * im) / jnp.sqrt(totals[:, 2] * totals[:, 3] + 1e-06)
    ifg[:, 0] = jnp.where(live, re / 451.0, 0.0)
    ifg[:, 1] = jnp.where(live, im / 451.0, 0.0)
    coh[...] = jnp.where(live, value, 0.0)


def on_device(acquisitions, reference_index, secondary_index, pair_count):
    view = acquisitions.reshape(ACQ, 2, LINES, TILES, 128)
    view = with_layout_constraint(view, Layout((0, 2, 3, 1, 4)))
    view = view.transpose(0, 2, 3, 1, 4)
    hbm = pl.BlockSpec(memory_space=pltpu.HBM)
    vmem = pl.BlockSpec(memory_space=pltpu.VMEM)
    dma = pltpu.SemaphoreType.DMA
    totals = pl.pallas_call(
        kernel,
        out_shape=pltpu.VMEM((SLOTS, 4, 4, 128), F32),
        in_specs=[hbm] * 3,
        out_specs=vmem,
        scratch_shapes=[
            pltpu.VMEM((ACQ, LINES, WIDE, 2, 128), BF16),
            pltpu.VMEM((EDGE, LINES, WIDE, 2, 128), BF16),
            pltpu.VMEM((ACQ * ROWS, 128), F32),
            pltpu.VMEM((EDGE * ROWS, 128), F32),
            pltpu.VMEM((128 * WIDE, 128), BF16),
            pltpu.VMEM((EARLY * 8 * PITCH, 128), F32),
            pltpu.VMEM((EARLY * 16, 128 * WIDE), BF16),
            pltpu.VMEM((EARLY, 8, 128), F32),
            pltpu.VMEM((LATE, 8, 128), F32),
            pltpu.VMEM((3, 16, 4, 128), F32),
            pltpu.VMEM((3, 16, 128), F32),
            pltpu.VMEM((2, 16, 4, 128), F32),
            pltpu.VMEM((3, 16, 128), F32),
            pltpu.VMEM((2, 8, 4, 128), F32),
            pltpu.VMEM((2, 8, 128), F32),
            pltpu.VMEM((8, 4, 128), F32),
            pltpu.VMEM((8, 128), F32),
        ] + [pltpu.SMEM((SLOTS,), jnp.int32)] * 6 + [
            dma((3,)), dma((EDGE,)), dma((EDGE,)), dma((3,)), dma((3,)),
            dma((4,)), dma((4,)), dma((5,)), dma((5,)), dma((2,)), dma((2,)),
            pltpu.SemaphoreType.REGULAR,
        ],
        compiler_params=pltpu.CompilerParams(
            collective_id=0, has_side_effects=True, vmem_limit_bytes=60 * 2**20
        ),
    )(view, reference_index, secondary_index)
    return pl.pallas_call(
        finish,
        out_shape=(
            jax.ShapeDtypeStruct((SLOTS, 2, 4, 128), F32),
            jax.ShapeDtypeStruct((SLOTS, 4, 128), F32),
        ),
        in_specs=[vmem, vmem],
        out_specs=(vmem, vmem),
        compiler_params=pltpu.CompilerParams(vmem_limit_bytes=2**20),
    )(totals, pair_count.reshape(1, 1))


def solution(mesh):
    return jax.shard_map(
        on_device,
        mesh=mesh,
        in_specs=(P("pair", None, "az", "rg"), P("pair"), P("pair"), P("pair")),
        out_specs=(P("pair", None, "az", "rg"), P("pair", "az", "rg")),
        check_vma=False,
    )
```

```python
import functools

import jax
import jax.numpy as jnp
from jax import lax
from jax.experimental import pallas as pl
from jax.experimental.layout import Layout, with_layout_constraint
from jax.experimental.pallas import tpu as pltpu
from jax.sharding import PartitionSpec as P

MESH = pl.DeviceIdType.MESH
ACQ = 16
SLOTS = 4
LINES = 20
TILES = 20
WIDE = TILES + 1
COMBOS = ((1, 0), (1, 1), (1, 2), (2, 0), (2, 1), (3, 0))
FORWARD = 5
TURN = 16
EDGE = 3
CROSS = 2 * 3 * SLOTS
EARLY = CROSS + ACQ
LATE = 2 * len(COMBOS)
PITCH = 24
ROWS = LINES * WIDE * 2
F32 = jnp.float32
BF16 = jnp.bfloat16


def kernel(
    acq, ref_hbm, sec_hbm, totals,
    block, edge, wide, wide_edge, table,
    sums, lhs, early, late,
    out_a, out_b, in_a, in_b, late_a, late_b, in_late_a, in_late_b,
    ref_own, sec_own, ref_prev, sec_prev, ref_next, sec_next,
    local_sem, slab_send, slab_recv,
    tile_send, tile_recv, index_send, index_recv, back_send, back_recv, late_send, late_recv, ready,
):
    d = lax.axis_index("pair")
    az = lax.axis_index("az")
    rg = lax.axis_index("rg")
    n = lax.axis_size("pair")
    oaz = 1 - az
    org = 1 - rg

    def at(step):
        return lax.rem(d + step + n, n)

    prev, nxt = at(-1), at(1)
    base = ACQ * d
    has_prev, has_next = d > 0, d < n - 1
    upper = az == 0

    own = [
        pltpu.make_async_copy(acq, block.at[:, :, pl.ds(0, TILES)], local_sem.at[0]),
        pltpu.make_async_copy(ref_hbm, ref_own, local_sem.at[1]),
        pltpu.make_async_copy(sec_hbm, sec_own, local_sem.at[2]),
    ]
    for copy in own:
        copy.start()

    barrier = pltpu.get_barrier_semaphore()
    def greet(semaphore, peers):
        for peer in peers:
            pl.semaphore_signal(semaphore, inc=1, device_id=peer, device_id_type=MESH)

    greet(barrier, [(d, az, org), (d, oaz, rg)])

    @pl.when(has_prev)
    def _():
        greet(barrier, [(prev, az, rg), (prev, az, org), (prev, oaz, rg)])

    pl.semaphore_wait(barrier, jnp.where(has_next, 5, 2))

    @pl.when(has_next)
    def _():
        greet(ready, [(nxt, az, rg), (nxt, oaz, rg), (nxt, az, org)])

    def remote(src, dst, send, recv, device):
        return pltpu.make_async_remote_copy(
            src_ref=src, dst_ref=dst, send_sem=send, recv_sem=recv,
            device_id=device, device_id_type=MESH,
        )

    class Toward:
        def __init__(self, step, *parts):
            self.copy = remote(*parts)
            self.sends, self.receives = (
                (has_next, has_prev) if step > 0 else (has_prev, has_next)
            )

        def start(self):
            pl.when(self.sends)(self.copy.start)

        def wait_send(self):
            pl.when(self.sends)(self.copy.wait_send)

        def wait_recv(self):
            pl.when(self.receives)(self.copy.wait_recv)

        def wait(self):
            self.wait_send()
            self.wait_recv()

    forward = functools.partial(Toward, 1)
    backward = functools.partial(Toward, -1)

    @pl.when(jnp.logical_not(has_prev))
    def _():
        for ref in (in_a.at[0], in_b.at[0], in_late_a, in_late_b):
            ref[...] = jnp.zeros(ref.shape, F32)
        for k in range(SLOTS):
            ref_prev[k] = 0
            sec_prev[k] = 0

    @pl.when(jnp.logical_not(has_next))
    def _():
        for ref in (in_a.at[1], in_b.at[2]):
            ref[...] = jnp.zeros(ref.shape, F32)
        for k in range(SLOTS):
            ref_next[k] = 0
            sec_next[k] = 0

    slabs = [
        forward(acq.at[ACQ - 2], edge.at[0, :, pl.ds(0, TILES)],
               slab_send.at[0], slab_recv.at[0], (nxt, az, rg)),
        forward(acq.at[ACQ - 1], edge.at[1, :, pl.ds(0, TILES)],
               slab_send.at[1], slab_recv.at[1], (nxt, az, rg)),
        backward(acq.at[0], edge.at[2, :, pl.ds(0, TILES)],
               slab_send.at[2], slab_recv.at[2], (prev, az, rg)),
    ]
    border = (TILES - 1) * org
    tiles = [
        remote(acq.at[:, :, border], block.at[:, :, TILES],
               tile_send.at[0], tile_recv.at[0], (d, az, org)),
        forward(acq.at[pl.ds(ACQ - 2, 2), :, border], edge.at[pl.ds(0, 2), :, TILES],
               tile_send.at[1], tile_recv.at[1], (nxt, az, org)),
        backward(acq.at[0, :, border], edge.at[2, :, TILES],
               tile_send.at[2], tile_recv.at[2], (prev, az, org)),
    ]
    indices = [
        backward(ref_hbm, ref_next, index_send.at[0], index_recv.at[0], (prev, az, rg)),
        backward(sec_hbm, sec_next, index_send.at[1], index_recv.at[1], (prev, az, rg)),
        forward(ref_hbm, ref_prev, index_send.at[2], index_recv.at[2], (nxt, az, rg)),
        forward(sec_hbm, sec_prev, index_send.at[3], index_recv.at[3], (nxt, az, rg)),
    ]
    for copy in indices[2:]:
        copy.start()
    tiles[0].start()
    for a in (1, 0):
        slabs[a].start()
    tiles[1].start()

    col = lax.broadcasted_iota(jnp.int32, (128, 128), 1) * 20
    row = lax.broadcasted_iota(jnp.int32, (128, 128), 0)
    for t in range(WIDE):
        sample = row + 128 * t
        if t == TILES:
            sample = sample - (128 * WIDE) * rg
        inside = (sample >= col - 10) & (sample <= col + 30)
        table[pl.ds(128 * t, 128), :] = jnp.where(inside, 1.0, 0.0).astype(BF16)

    def line(ref, a, l):
        start = a * ROWS + l * (2 * WIDE)
        return (
            ref[pl.ds(start, WIDE, stride=2), :],
            ref[pl.ds(start + 1, WIDE, stride=2), :],
        )

    def put(plane, window, value):
        start = pl.multiple_of((plane * 8 + window) * PITCH, 8)
        sums[pl.ds(start, WIDE), :] = value

    def line_sums(plane, get):
        def add(*terms):
            total = terms[0]
            for term in terms[1:]:
                total = tuple(x + y for x, y in zip(total, term))
            return total

        def store(window, value):
            for i, v in enumerate(value):
                put(plane + i, window, v)

        l2 = None
        s0 = add(get(0), get(1))
        l2 = get(2)
        up = add(s0, l2)
        s3 = add(get(3), get(4), get(5), get(6))
        l7 = get(7)
        m1 = add(s3, l7)
        store(0, add(up, m1))
        s8 = add(get(8), get(9), get(10), get(11))
        l12 = get(12)
        m2 = add(s8, l12)
        store(1, add(l2, m1, m2))
        s13 = add(get(13), get(14), get(15), get(16))
        l17 = get(17)
        m3 = add(s13, l17)
        store(2, add(l7, m2, m3))
        down = add(l17, get(18), get(19))
        store(3, add(l12, s13, down))
        store(4, tuple(jnp.where(upper, x, y) for x, y in zip(down, up)))

    def power(plane, a):
        def get(l):
            x, y = line(wide, a, l)
            return (x * x + y * y,)
        line_sums(plane, get)

    def cross(plane, one, a, two, b):
        def get(l):
            xr, yr = line(one, a, l)
            xs, ys = line(two, b, l)
            return (xr * xs + yr * ys, yr * xs - xr * ys)
        line_sums(plane, get)

    def range_sums(first, planes, result):
        rows = planes * 8
        for t in range(WIDE):
            v = sums[pl.ds(first * 8 * PITCH + t, rows, stride=PITCH), :]
            hi = v.astype(BF16)
            lo = (v - hi.astype(F32)).astype(BF16)
            lhs[pl.ds(0, rows), pl.ds(128 * t, 128)] = hi
            lhs[pl.ds(rows, rows), pl.ds(128 * t, 128)] = lo
        both = jnp.dot(lhs[pl.ds(0, 2 * rows), :], table[...], preferred_element_type=F32)
        total = both[:rows] + both[rows:]
        result[pl.ds(first, planes)] = total.reshape(planes, 8, 128)

    def send_back():
        pl.when(has_prev)(lambda: pl.semaphore_wait(ready, 3))
        for copy in indices[:2]:
            copy.start()
        slabs[2].start()
        tiles[2].start()

    soon = lax.rem(d, 2) == 1
    pl.when(soon)(send_back)

    own[0].wait()
    tiles[0].wait_recv()

    def widen(a, carry):
        start = pl.multiple_of(a * ROWS, 8)
        wide[pl.ds(start, ROWS), :] = block[a].reshape(ROWS, 128).astype(F32)
        return carry

    lax.fori_loop(0, ACQ, widen, 0)

    def power_step(a, carry):
        power(CROSS + a, a)
        return carry

    lax.fori_loop(0, ACQ, power_step, 0)

    for copy in own[1:]:
        copy.wait()
    names = [(ref_prev, sec_prev), (ref_own, sec_own), (ref_next, sec_next)]

    def clip(i):
        return jnp.clip(i, 0, ACQ - 1)

    def group(g):
        refs, secs = names[g]

        def cross_step(k, carry):
            cross(2 * (SLOTS * g + k), wide, clip(refs[k] - base), wide, clip(secs[k] - base))
            return carry

        lax.fori_loop(0, SLOTS, cross_step, 0)

    group(1)
    pl.when(jnp.logical_not(soon))(send_back)
    for copy in indices[2:]:
        copy.wait_recv()
    group(0)
    for copy in indices[:2]:
        copy.wait_recv()
    group(2)

    range_sums(0, EARLY, early)

    zero = jnp.zeros((8, 128), F32)

    def collect(g, behind):
        refs, secs = names[g]
        for k in range(SLOTS):
            r = refs[k] - base
            s = secs[k] - base
            has_r = (r >= 0) & (r < ACQ)
            has_s = (s >= 0) & (s < ACQ)
            reach = ((r == -1) | (r == -2)) & has_s
            combo = jnp.clip(jnp.where(r == -1, s, s + 3), 0, FORWARD - 1)
            for c in range(4):
                if c < 2:
                    value = jnp.where(has_r & has_s, early[2 * (SLOTS * g + k) + c], zero)
                    if behind:
                        value = value + jnp.where(reach, late[2 * combo + c], zero)
                elif c == 2:
                    value = jnp.where(has_r, early[CROSS + clip(r)], zero)
                else:
                    value = jnp.where(has_s, early[CROSS + clip(s)], zero)
                out_a[g, 4 * k + c] = value[0:4]
                out_b[g, pl.ds(4 * k + c, 1), :] = value[4:5]

    collect(2, False)
    backs = [
        forward(out_a.at[2], in_a.at[0], back_send.at[0], back_recv.at[0], (nxt, az, rg)),
        forward(out_b.at[2], in_b.at[0], back_send.at[1], back_recv.at[1], (nxt, oaz, rg)),
        backward(out_a.at[0], in_a.at[1], back_send.at[2], back_recv.at[2], (prev, az, rg)),
        backward(out_b.at[0], in_b.at[2], back_send.at[3], back_recv.at[3], (prev, oaz, rg)),
        remote(out_b.at[1], in_b.at[1], back_send.at[4], back_recv.at[4], (d, oaz, rg)),
    ]
    for copy in backs[:2]:
        copy.start()

    def widen_edge(a):
        slabs[a].wait_recv()
        wide_edge[pl.ds(a * ROWS, ROWS), :] = edge[a].reshape(ROWS, 128).astype(F32)

    lates = [
        forward(late_a.at[1], in_late_a, late_send.at[0], late_recv.at[0], (nxt, az, rg)),
        forward(late_b.at[1], in_late_b, late_send.at[1], late_recv.at[1], (nxt, oaz, rg)),
    ]

    def reach_back():
        tiles[1].wait_recv()
        for a, far in ((1, 1), (0, 2)):
            widen_edge(a)
            for i, (r, s) in enumerate(COMBOS[:FORWARD]):
                if r == far:
                    cross(2 * i, wide_edge, a, wide, s)
        range_sums(0, 2 * FORWARD, late)
        collect(0, True)
        for copy in backs[2:4]:
            copy.start()
        collect(1, True)

    def reach_ahead():
        tiles[2].wait_recv()
        widen_edge(2)
        cross(2 * FORWARD, wide, ACQ - 3, wide_edge, 2)
        range_sums(2 * FORWARD, 2, late)
        for g in (2, 1):
            refs, secs = names[g]
            for k in range(SLOTS):
                reach = (refs[k] - base == ACQ - 3) & (secs[k] - base == ACQ)
                for c in range(2):
                    value = jnp.where(reach, late[2 * FORWARD + c], zero)
                    late_a[g - 1, 2 * k + c] = value[0:4]
                    late_b[g - 1, pl.ds(2 * k + c, 1), :] = value[4:5]
            if g == 2:
                for copy in lates:
                    copy.start()

    turned = lax.rem(d, TURN) == TURN - 1
    pl.when(turned)(reach_ahead)
    reach_back()
    pl.when(jnp.logical_not(turned))(reach_ahead)

    for k in range(SLOTS):
        for c in range(2):
            i, j = 4 * k + c, 2 * k + c
            out_a[1, i] = out_a[1, i] + late_a[0, j]
            out_b[1, pl.ds(i, 1), :] = out_b[1, pl.ds(i, 1), :] + late_b[0, pl.ds(j, 1), :]
    backs[4].start()
    for copy in tiles + indices + slabs:
        copy.wait_send()
    for copy in backs + lates:
        copy.wait()

    window = lax.broadcasted_iota(jnp.int32, (4, 128), 0)
    shared = window == 3 * oaz
    for k in range(SLOTS):
        for c in range(4):
            i = 4 * k + c
            rim = in_b[0, pl.ds(i, 1), :] + in_b[1, pl.ds(i, 1), :] + in_b[2, pl.ds(i, 1), :]
            body = out_a[1, i] + in_a[0, i] + in_a[1, i]
            if c < 2:
                j = 2 * k + c
                rim = rim + in_late_b[pl.ds(j, 1), :]
                body = body + in_late_a[j]
            totals[k, c] = body + jnp.where(shared, rim, 0.0)


def finish(totals, count, ifg, coh):
    slot = lax.broadcasted_iota(jnp.int32, (SLOTS, 4, 128), 0)
    live = slot < count[...].reshape(1, 1, 1)
    re, im = totals[:, 0], totals[:, 1]
    value = jnp.sqrt(re * re + im * im) / jnp.sqrt(totals[:, 2] * totals[:, 3] + 1e-06)
    ifg[:, 0] = jnp.where(live, re / 451.0, 0.0)
    ifg[:, 1] = jnp.where(live, im / 451.0, 0.0)
    coh[...] = jnp.where(live, value, 0.0)


def on_device(acquisitions, reference_index, secondary_index, pair_count):
    view = acquisitions.reshape(ACQ, 2, LINES, TILES, 128)
    view = with_layout_constraint(view, Layout((0, 2, 3, 1, 4)))
    view = view.transpose(0, 2, 3, 1, 4)
    hbm = pl.BlockSpec(memory_space=pltpu.HBM)
    vmem = pl.BlockSpec(memory_space=pltpu.VMEM)
    dma = pltpu.SemaphoreType.DMA
    totals = pl.pallas_call(
        kernel,
        out_shape=pltpu.VMEM((SLOTS, 4, 4, 128), F32),
        in_specs=[hbm] * 3,
        out_specs=vmem,
        scratch_shapes=[
            pltpu.VMEM((ACQ, LINES, WIDE, 2, 128), BF16),
            pltpu.VMEM((EDGE, LINES, WIDE, 2, 128), BF16),
            pltpu.VMEM((ACQ * ROWS, 128), F32),
            pltpu.VMEM((EDGE * ROWS, 128), F32),
            pltpu.VMEM((128 * WIDE, 128), BF16),
            pltpu.VMEM((EARLY * 8 * PITCH, 128), F32),
            pltpu.VMEM((EARLY * 16, 128 * WIDE), BF16),
            pltpu.VMEM((EARLY, 8, 128), F32),
            pltpu.VMEM((LATE, 8, 128), F32),
            pltpu.VMEM((3, 16, 4, 128), F32),
            pltpu.VMEM((3, 16, 128), F32),
            pltpu.VMEM((2, 16, 4, 128), F32),
            pltpu.VMEM((3, 16, 128), F32),
            pltpu.VMEM((2, 8, 4, 128), F32),
            pltpu.VMEM((2, 8, 128), F32),
            pltpu.VMEM((8, 4, 128), F32),
            pltpu.VMEM((8, 128), F32),
        ] + [pltpu.SMEM((SLOTS,), jnp.int32)] * 6 + [
            dma((3,)), dma((EDGE,)), dma((EDGE,)), dma((3,)), dma((3,)),
            dma((4,)), dma((4,)), dma((5,)), dma((5,)), dma((2,)), dma((2,)),
            pltpu.SemaphoreType.REGULAR,
        ],
        compiler_params=pltpu.CompilerParams(
            collective_id=0, has_side_effects=True, vmem_limit_bytes=60 * 2**20
        ),
    )(view, reference_index, secondary_index)
    return pl.pallas_call(
        finish,
        out_shape=(
            jax.ShapeDtypeStruct((SLOTS, 2, 4, 128), F32),
            jax.ShapeDtypeStruct((SLOTS, 4, 128), F32),
        ),
        in_specs=[vmem, vmem],
        out_specs=(vmem, vmem),
        compiler_params=pltpu.CompilerParams(vmem_limit_bytes=2**20),
    )(totals, pair_count.reshape(1, 1))


def solution(mesh):
    return jax.shard_map(
        on_device,
        mesh=mesh,
        in_specs=(P("pair", None, "az", "rg"), P("pair"), P("pair"), P("pair")),
        out_specs=(P("pair", None, "az", "rg"), P("pair", "az", "rg")),
        check_vma=False,
    )
```
